512 devices in a mesh: slab: 16 (over z_lo, y), ctrl: 32 (over z_hi, x, core).
Axes of the slice: x: 4, y: 4, z: 16 (z_hi: 4, z_lo: 4; z = z_hi * 4 + z_lo), core: 2. Of those that a mesh axis runs over, the one named last changes fastest.
Arguments:
- value: float32 [256, 128, 128], P('slab'), may hold values from -6 to 6
- speed: float32 [256, 128, 128], P('slab'), may hold values from 0.25 to 1
- reward: bfloat16 [64, 256, 128, 128], P('ctrl', 'slab'), may hold values from -0.8984375 to 0.8984375
- ctrl_set: int32 [64], P('ctrl'), may hold values from 0 to 15, as said below
- drift_sets: float32 [16, 3], replicated, may hold values from -0.08 to 0.08
- diffusion_sets: float32 [16, 3], replicated, may hold values from 0.03 to 0.12
Outputs:
- value_out: float32 [256, 128, 128], P('slab')
The draws below stay inside these ranges and needn't reach their ends.
Inputs may be any that keep to these rules, and one draw needn't show every extreme that they name: `ctrl_set`: each of the 16 sets is named by exactly 4 controls.
All inputs are finite; a program needn't handle non-finite values.
Results may differ from the reference program's by a relative error of at most 0.0014.
Values may be sent and summed in bfloat16 or wider, within the bound.
A program may use at most 64 MiB of HBM per device.

```python
import jax
import jax.numpy as jnp
from jax import lax

NY = 128
NZ = 128
SETS = 16
SUBSTEPS = 3
OUTER = 2
NX = 256
CONTROLS = 64


def draw_ctrl_set(key, part):
    return (jax.random.permutation(jax.random.fold_in(key, 7), CONTROLS) % SETS).astype(jnp.int32)


def block_scale(own_key, extent, cuts, smallest, largest):
    loudness, own = 1.0, jax.random.fold_in(own_key, 6)
    for dim, parts in cuts:
        draws = jnp.exp(jax.random.uniform(jax.random.fold_in(own, dim), (parts,), jnp.float32, smallest / len(cuts), largest / len(cuts)))
        loudness = loudness * jnp.repeat(draws, extent[dim] // parts).reshape([-1 if axis == dim else 1 for axis in range(len(extent))])
    return loudness


def normal_values(own_key, dims, spread, bound, shards=(), kind=jnp.bfloat16):
    array = jax.random.normal(own_key, dims, jnp.float32) * spread
    if len(shards) > 0:
        array = block_scale(own_key, dims, shards, -0.22, 0.18) * array
    return jnp.clip(array, min=-bound, max=bound).astype(kind)


def setup_inputs(seed: int = 0) -> dict:
    arg_keys = jax.random.split(jax.random.key(seed), 7)
    return {
        "value": normal_values(arg_keys[0], (NX, NY, NZ), 1.0, 6.0, ((0, 16),), jnp.float32),
        "speed": jnp.clip(0.25 + 0.75 * jax.random.uniform(arg_keys[1], (NX, NY, NZ), jnp.float32) ** block_scale(arg_keys[1], (NX, NY, NZ), ((0, 16),), -0.2, 0.2), 0.25, 1.0),
        "reward": normal_values(arg_keys[2], (CONTROLS, NX, NY, NZ), 0.15, 0.8984375, ((0, 32), (1, 16))),
        "ctrl_set": draw_ctrl_set(jax.random.fold_in(arg_keys[6], 71), 0),
        "drift_sets": jnp.clip(jax.random.uniform(arg_keys[4], (SETS, 3), jnp.float32, -0.08, 0.08), -0.08, 0.08),
        "diffusion_sets": jnp.clip(jax.random.uniform(arg_keys[5], (SETS, 3), jnp.float32, 0.03, 0.12), 0.03, 0.12),
    }


def upshift(field, axis):
    widths = [(0, 0)] * 4
    widths[axis] = (0, 1)
    padded = jnp.pad(field, widths)
    return lax.slice_in_dim(padded, 1, padded.shape[axis], axis=axis)


def downshift(field, axis):
    widths = [(0, 0)] * 4
    widths[axis] = (1, 0)
    padded = jnp.pad(field, widths)
    return lax.slice_in_dim(padded, 0, padded.shape[axis] - 1, axis=axis)


def advance(padded, speed_part, reward_part, diffusion, drift):
    center = padded[:, 1:-1]
    ahead = [padded[:, 2:], upshift(center, 2), upshift(center, 3)]
    behind = [padded[:, :-2], downshift(center, 2), downshift(center, 3)]
    total = center + reward_part
    for axis_num in range(3):
        rate = diffusion[:, axis_num][:, None, None, None]
        flow = drift[:, axis_num][:, None, None, None] * speed_part[None]
        forward = ahead[axis_num] - center
        backward = center - behind[axis_num]
        total = total + rate * (forward - backward) + jnp.maximum(flow, 0.0) * forward + jnp.minimum(flow, 0.0) * backward
    return total


def reference(value, speed, reward, ctrl_set, drift_sets, diffusion_sets):
    diffusion = diffusion_sets[ctrl_set]
    drift = drift_sets[ctrl_set]
    current = value
    for outer_round in range(OUTER):
        def visit(best, inputs):
            reward_one, diffusion_one, drift_one = inputs
            field = current[None]
            for substep in range(SUBSTEPS):
                padded = jnp.pad(field, ((0, 0), (1, 1), (0, 0), (0, 0)))
                field = advance(padded, speed, reward_one.astype(jnp.float32)[None], diffusion_one[None], drift_one[None])
            return jnp.maximum(best, field[0]), None

        start = jnp.full(current.shape, -jnp.inf, dtype=current.dtype)
        current, unused = lax.scan(visit, start, (reward, diffusion, drift))
    return current
```

```python
import functools

import jax
import jax.numpy as jnp
from jax import lax
from jax.experimental import pallas as pl
from jax.experimental.pallas import tpu as pltpu
from jax.sharding import PartitionSpec as P

MESH = pl.DeviceIdType.MESH
F32 = jnp.float32
I16 = jnp.int16
OUTER = 2
NP = 16
NY = 128
NZ = 128
BLK = 32
KEY = 32767.0 / 11.45**0.25
SKEY = 32767.0 / 0.376
CHUNKS = ((0, 5), (5, 5), (10, 6))


def encode(v):
    root = lax.rsqrt(lax.rsqrt(jnp.maximum(jnp.abs(v), 1e-30)))
    size = root * KEY + 0.5
    return jnp.where(v < 0.0, -size, size).astype(jnp.int32).astype(I16)


def decode(code):
    g = code.astype(jnp.int32).astype(F32) * (1.0 / KEY)
    return (g * jnp.abs(g)) * (g * g)


def encode_speed(s):
    t = (s - 0.625) * SKEY
    return jnp.where(t < 0.0, t - 0.5, t + 0.5).astype(jnp.int32).astype(I16)


def decode_speed(code):
    return code.astype(jnp.int32).astype(F32) * (1.0 / SKEY) + 0.625


def top(*codes):
    best = codes[0].astype(jnp.int32).astype(F32)
    for code in codes[1:]:
        best = jnp.maximum(best, code.astype(jnp.int32).astype(F32))
    return best.astype(jnp.int32).astype(I16)


def plane_of(pos):
    return pos + 3


def edge_plane(j):
    return j + (j // 3) * 10


def kernel(
    cset, drift, diff, value, speed, reward, out,
    u, sp, rw, f1, f2, enc, rc, hc, rx, hx, rz, res, vst, hv, sst, hs,
    load_sem, halo_ss, halo_rs, core_ss, core_rs, x_ss, x_rs, z_ss, z_rs, xa_ss, xa_rs, ca_ss, ca_rs,
):
    slab = lax.axis_index("slab")
    ctrl = lax.axis_index("ctrl")
    core = lax.rem(ctrl, 2)
    x = lax.rem(ctrl // 2, 4)
    z = ctrl // 8

    def at(z, x, core):
        return {"slab": slab, "ctrl": (z * 4 + x) * 2 + core}

    mate = at(z, x, 1 - core)
    xs = [lax.rem(x + k, 4) for k in (1, 2, 3)]
    x_peers = [at(z, xk, core) for xk in xs]
    z_peers = [at(lax.rem(z + k, 4), x, core) for k in (1, 2, 3)]
    below = {"slab": lax.rem(slab + 15, 16), "ctrl": ctrl}
    above = {"slab": lax.rem(slab + 1, 16), "ctrl": ctrl}
    peers = [mate] + x_peers + z_peers + [below, above]

    barrier = pltpu.get_barrier_semaphore()
    for peer in peers:
        pl.semaphore_signal(barrier, inc=1, device_id=peer, device_id_type=MESH)

    loads = [
        pltpu.make_async_copy(value, u.at[3 : 3 + NP, 8 : 8 + NY], load_sem.at[0]),
        pltpu.make_async_copy(speed, sp.at[2 : 2 + NP], load_sem.at[1]),
        pltpu.make_async_copy(reward, rw.at[:, 2 : 2 + NP], load_sem.at[2]),
    ]
    for load in loads:
        load.start()

    strip = jnp.zeros((8, NZ), F32)

    def clear(i, carry):
        u[i, 0:8] = strip
        u[i, 8 + NY : 16 + NY] = strip
        return carry

    lax.fori_loop(0, NP + 6, clear, 0)

    def clear_one(i, carry):
        for c in range(2):
            f1[c, i, 0:8] = strip
            f1[c, i, 8 + NY : 16 + NY] = strip
        return carry

    lax.fori_loop(0, NP + 4, clear_one, 0)

    def clear_two(i, carry):
        for c in range(2):
            f2[c, i, 0:8] = strip
            f2[c, i, 8 + NY : 16 + NY] = strip
        return carry

    lax.fori_loop(0, NP + 2, clear_two, 0)

    a, e, pos_b, mid, total = [], [], [], [], []
    for c in range(2):
        k = cset[c]
        a.append([diff[k, d] for d in range(3)])
        b = [drift[k, d] for d in range(3)]
        e.append([jnp.abs(bd) for bd in b])
        pos_b.append(b)
        mid.append(1.0 - 2.0 * (a[c][0] + a[c][1] + a[c][2]))
        total.append(e[c][0] + e[c][1] + e[c][2])

    lane = lax.broadcasted_iota(jnp.int32, (BLK, NZ), 1)
    not_last = lane < NZ - 1
    not_first = lane > 0

    def neighbours(src, p, r0):
        here = src[p, 8 + r0 : 8 + r0 + BLK]
        ahead = [
            src[p + 1, 8 + r0 : 8 + r0 + BLK],
            src[p, 9 + r0 : 9 + r0 + BLK],
            jnp.where(not_last, pltpu.roll(here, NZ - 1, 1), 0.0),
        ]
        behind = [
            src[p - 1, 8 + r0 : 8 + r0 + BLK],
            src[p, 7 + r0 : 7 + r0 + BLK],
            jnp.where(not_first, pltpu.roll(here, 1, 1), 0.0),
        ]
        sums = [f + g for f, g in zip(ahead, behind)]
        return here, ahead, behind, sums

    def advance(step, p, r0):
        pace = sp[p + 2, r0 : r0 + BLK]
        if step == 0:
            shared = neighbours(u, p + 3, r0)
        results = []
        for c in range(2):
            if step == 0:
                here, ahead, behind, sums = shared
            elif step == 1:
                here, ahead, behind, sums = neighbours(f1.at[c], p + 2, r0)
            else:
                here, ahead, behind, sums = neighbours(f2.at[c], p + 1, r0)
            pay = rw[c, p + 2, r0 : r0 + BLK].astype(F32)
            wind = [
                e[c][d] * jnp.where(jnp.full((BLK, NZ), pos_b[c][d], F32) > 0.0, ahead[d], behind[d])
                for d in range(3)
            ]
            spread = (a[c][0] * sums[0] + a[c][1] * sums[1]) + (a[c][2] * sums[2] + mid[c] * here)
            flow = (wind[0] + wind[1]) + (wind[2] - total[c] * here)
            results.append((spread + pay) + pace * flow)
        return results

    def inside(p):
        lost = jnp.logical_or(jnp.logical_and(p < 0, slab == 0), jnp.logical_and(p >= NP, slab == 15))
        return jnp.where(lost, jnp.float32(0.0), jnp.float32(1.0))

    def sweep(step, low, high, o, edge):
        def body(j, carry):
            if edge:
                p = j + (step - 2) + (j // 3) * (14 - 2 * step)
                keep = inside(p)
            else:
                p = j
            for r0 in range(0, NY, BLK):
                both = advance(step, p, r0)
                if step < 2:
                    dst, off = (f1, 2) if step == 0 else (f2, 1)
                    for c in range(2):
                        dst[c, p + off, 8 + r0 : 8 + r0 + BLK] = both[c] * keep if edge else both[c]
                else:
                    code = encode(jnp.maximum(both[0], both[1]))
                    pos = 10 + j if edge else p - 3
                    for i in range(BLK // 16):
                        h, q = divmod(r0 // 16 + i, 4)
                        enc[o, h, q, pos] = code[16 * i : 16 * i + 16]
            return carry

        lax.fori_loop(low, high, body, 0)

    def remote(src, dst, ss, rs, peer):
        return pltpu.make_async_remote_copy(
            src_ref=src, dst_ref=dst, send_sem=ss, recv_sem=rs, device_id=peer, device_id_type=MESH
        )

    sent = []

    def start(copies):
        for copy in copies:
            copy.start()
            sent.append(copy)
        return copies

    def arrived(copies):
        for copy in copies:
            copy.wait_recv()

    flight = {}

    def each(ci, body):
        first, count = CHUNKS[ci]

        def step(i, carry):
            body(i)
            return carry

        lax.fori_loop(first, first + count, step, 0)

    def cut(ci):
        first, count = CHUNKS[ci]
        return slice(first, first + count)

    def send_core(o, ci):
        w = cut(ci)
        flight["core", o, ci] = start(
            [remote(enc.at[o, 1 - core, :, w], rc.at[o, :, w], core_ss.at[o, ci], core_rs.at[o, ci], mate)]
        )

    def merge_core(o, ci):
        w = cut(ci)
        arrived(flight["core", o, ci])

        def body(i):
            for q in range(4):
                hc[o, q, i] = top(enc[o, core, q, i], rc[o, q, i])

        each(ci, body)
        flight["x", o, ci] = start(
            [
                remote(hc.at[o, xs[k], w], rx.at[o, k, w], x_ss.at[o, ci, k], x_rs.at[o, ci, k], x_peers[k])
                for k in range(3)
            ]
        )

    def merge_x(o, ci):
        w = cut(ci)
        arrived(flight["x", o, ci])

        def body(i):
            hx[o, i] = top(hc[o, x, i], rx[o, 0, i], rx[o, 1, i], rx[o, 2, i])

        each(ci, body)
        flight["z", o, ci] = start(
            [
                remote(hx.at[o, w], rz.at[o, k, w], z_ss.at[o, ci, k], z_rs.at[o, ci, k], z_peers[k])
                for k in range(3)
            ]
        )

    def merge_z(o, ci):
        w = cut(ci)
        arrived(flight["z", o, ci])

        def body(i):
            res[o, core, x, i] = top(hx[o, i], rz[o, 0, i], rz[o, 1, i], rz[o, 2, i])

        each(ci, body)
        mine = res.at[o, core, x, w]
        flight["xa", o, ci] = start(
            [remote(mine, mine, xa_ss.at[o, ci, k], xa_rs.at[o, ci, k], x_peers[k]) for k in range(3)]
        )

    def gather_x(o, ci):
        arrived(flight["xa", o, ci])
        half = res.at[o, core, :, cut(ci)]
        flight["ca", o, ci] = start([remote(half, half, ca_ss.at[o, ci], ca_rs.at[o, ci], mate)])

    def finish(o, ci):
        arrived(flight["ca", o, ci])

        def body(i):
            p = i + 3 if ci < 2 else edge_plane(i - 10)
            for h in range(2):
                for q in range(4):
                    row = 64 * h + 16 * q
                    if o == 0:
                        u[p + 3, 8 + row : 24 + row] = decode(res[o, h, q, i])
                    else:
                        out[p, row : row + 16] = res[o, h, q, i]

        each(ci, body)

    def send_halo(o, low, high):
        flight["halo", o] = start(
            [
                remote(low, hv.at[o, 1], halo_ss.at[o, 0], halo_rs.at[o, 0], below),
                remote(high, hv.at[o, 0], halo_ss.at[o, 1], halo_rs.at[o, 1], above),
            ]
        )

    def take_halo(o):
        arrived(flight["halo", o])

        def body(i, carry):
            for side in range(2):
                p = i - 3 if side == 0 else i + NP
                keep = inside(p)
                for h in range(2):
                    for q in range(4):
                        row = 8 + 64 * h + 16 * q
                        u[p + 3, row : row + 16] = decode(hv[o, side, h, q, i]) * keep
            return carry

        lax.fori_loop(0, 3, body, 0)

    loads[0].wait()

    def stage(i, carry):
        for side in range(2):
            p = i if side == 0 else i + NP - 3
            for h in range(2):
                for q in range(4):
                    row = 8 + 64 * h + 16 * q
                    vst[side, h, q, i] = encode(u[p + 3, row : row + 16])
        return carry

    lax.fori_loop(0, 3, stage, 0)
    loads[1].wait()

    def stage_speed(i, carry):
        for side in range(2):
            p = i if side == 0 else i + NP - 2
            for r0 in range(0, NY, BLK):
                sst[side, i, r0 : r0 + BLK] = encode_speed(sp[p + 2, r0 : r0 + BLK])
        return carry

    lax.fori_loop(0, 2, stage_speed, 0)
    loads[2].wait()

    sweep(0, 1, 15, 0, False)
    pl.semaphore_wait(barrier, len(peers))
    send_halo(0, vst.at[0], vst.at[1])
    extras = start(
        [
            remote(sst.at[0], hs.at[1], halo_ss.at[2, 0], halo_rs.at[2, 0], below),
            remote(sst.at[1], hs.at[0], halo_ss.at[2, 1], halo_rs.at[2, 1], above),
            remote(reward.at[:, 0:2], rw.at[:, NP + 2 : NP + 4], halo_ss.at[3, 0], halo_rs.at[3, 0], below),
            remote(reward.at[:, NP - 2 : NP], rw.at[:, 0:2], halo_ss.at[3, 1], halo_rs.at[3, 1], above),
        ]
    )
    sweep(1, 2, 14, 0, False)
    sweep(2, 3, 8, 0, False)
    send_core(0, 0)
    sweep(2, 8, 13, 0, False)
    send_core(0, 1)
    merge_core(0, 0)
    merge_core(0, 1)
    merge_x(0, 0)
    merge_x(0, 1)
    take_halo(0)
    arrived(extras)

    def take_speed(i, carry):
        for side in range(2):
            p = i - 2 if side == 0 else i + NP
            for r0 in range(0, NY, BLK):
                sp[p + 2, r0 : r0 + BLK] = decode_speed(hs[side, i, r0 : r0 + BLK])
        return carry

    lax.fori_loop(0, 2, take_speed, 0)
    sweep(0, 0, 6, 0, True)
    sweep(1, 0, 6, 0, True)
    sweep(2, 0, 6, 0, True)
    send_core(0, 2)
    merge_core(0, 2)
    merge_x(0, 2)
    for ci in range(2):
        merge_z(0, ci)
    for ci in range(2):
        gather_x(0, ci)
    for ci in range(2):
        finish(0, ci)
    merge_z(0, 2)
    gather_x(0, 2)
    finish(0, 2)

    send_halo(1, res.at[0, :, :, 10:13], res.at[0, :, :, 13:16])
    sweep(0, 1, 10, 1, False)
    sweep(1, 2, 9, 1, False)
    sweep(2, 3, 8, 1, False)
    send_core(1, 0)
    sweep(0, 10, 15, 1, False)
    merge_core(1, 0)
    sweep(1, 9, 14, 1, False)
    sweep(2, 8, 13, 1, False)
    send_core(1, 1)
    merge_x(1, 0)
    take_halo(1)
    sweep(0, 0, 6, 1, True)
    merge_core(1, 1)
    sweep(1, 0, 6, 1, True)
    sweep(2, 0, 6, 1, True)
    send_core(1, 2)
    merge_x(1, 1)
    merge_core(1, 2)
    merge_x(1, 2)
    for ci in range(3):
        merge_z(1, ci)
    for ci in range(3):
        gather_x(1, ci)
    for ci in range(3):
        finish(1, ci)
    for copy in sent:
        copy.wait_send()


def body(value, speed, reward, ctrl_set, drift_sets, diffusion_sets):
    smem = pl.BlockSpec(memory_space=pltpu.SMEM)
    hbm = pl.BlockSpec(memory_space=pl.ANY)
    dma = pltpu.SemaphoreType.DMA
    n = len(CHUNKS)
    code = pl.pallas_call(
        kernel,
        out_shape=jax.ShapeDtypeStruct((NP, NY, NZ), I16),
        in_specs=[smem, smem, smem, hbm, hbm, hbm],
        out_specs=pl.BlockSpec(memory_space=pltpu.VMEM),
        scratch_shapes=[
            pltpu.VMEM((NP + 6, NY + 16, NZ), F32),
            pltpu.VMEM((NP + 4, NY, NZ), F32),
            pltpu.VMEM((2, NP + 4, NY, NZ), jnp.bfloat16),
            pltpu.VMEM((2, NP + 4, NY + 16, NZ), F32),
            pltpu.VMEM((2, NP + 2, NY + 16, NZ), F32),
            pltpu.VMEM((2, 2, 4, NP, 16, NZ), I16),
            pltpu.VMEM((2, 4, NP, 16, NZ), I16),
            pltpu.VMEM((2, 4, NP, 16, NZ), I16),
            pltpu.VMEM((2, 3, NP, 16, NZ), I16),
            pltpu.VMEM((2, NP, 16, NZ), I16),
            pltpu.VMEM((2, 3, NP, 16, NZ), I16),
            pltpu.VMEM((2, 2, 4, NP, 16, NZ), I16),
            pltpu.VMEM((2, 2, 4, 3, 16, NZ), I16),
            pltpu.VMEM((2, 2, 2, 4, 3, 16, NZ), I16),
            pltpu.VMEM((2, 2, NY, NZ), I16),
            pltpu.VMEM((2, 2, NY, NZ), I16),
            dma((3,)),
            dma((4, 2)), dma((4, 2)),
            dma((2, n)), dma((2, n)),
            dma((2, n, 3)), dma((2, n, 3)),
            dma((2, n, 3)), dma((2, n, 3)),
            dma((2, n, 3)), dma((2, n, 3)),
            dma((2, n)), dma((2, n)),
        ],
        compiler_params=pltpu.CompilerParams(collective_id=0, has_side_effects=True),
        name="hjb",
    )(ctrl_set, drift_sets, diffusion_sets, value, speed, reward)
    return decode(code)


def solution(mesh):
    in_specs = (
        P("slab", None, None),
        P("slab", None, None),
        P("ctrl", "slab", None, None),
        P("ctrl"),
        P(),
        P(),
    )
    out_specs = P("slab", None, None)
    return jax.shard_map(body, mesh=mesh, in_specs=in_specs, out_specs=out_specs, check_vma=False)
```

```python
import functools

import jax
import jax.numpy as jnp
from jax import lax
from jax.experimental import pallas as pl
from jax.experimental.pallas import tpu as pltpu
from jax.sharding import PartitionSpec as P

MESH = pl.DeviceIdType.MESH
F32 = jnp.float32
I16 = jnp.int16
OUTER = 2
NP = 16
NY = 128
NZ = 128
BLK = 32
KEY = 32767.0 / 11.45**0.25
SKEY = 32767.0 / 0.376
CHUNKS = ((0, 4), (4, 6), (10, 3), (13, 3))
OFFSETS = tuple((dx, dc) for dx in (2, 1, 3, 0) for dc in range(2) if dx or dc)


def encode(v):
    root = lax.rsqrt(lax.rsqrt(jnp.maximum(jnp.abs(v), 1e-30)))
    size = root * KEY + 0.5
    return jnp.where(v < 0.0, -size, size).astype(jnp.int32).astype(I16)


def decode(code):
    g = code.astype(jnp.int32).astype(F32) * (1.0 / KEY)
    return (g * jnp.abs(g)) * (g * g)


def encode_speed(s):
    t = (s - 0.625) * SKEY
    return jnp.where(t < 0.0, t - 0.5, t + 0.5).astype(jnp.int32).astype(I16)


def decode_speed(code):
    return code.astype(jnp.int32).astype(F32) * (1.0 / SKEY) + 0.625


def top(*codes):
    best = codes[0].astype(jnp.int32).astype(F32)
    for code in codes[1:]:
        best = jnp.maximum(best, code.astype(jnp.int32).astype(F32))
    return best.astype(jnp.int32).astype(I16)


def pair_plane(j, base):
    return j + base + (j // 3) * (10 - 2 * base)


def kernel(
    cset_in, drift_in, diff_in, value, speed, reward, out,
    cset, drift, diff, u, sp, rw, f1, f2, enc, rx, hx, rz, res, vst, hv, sst, hs,
    load_sem, halo_ss, halo_rs, x_ss, x_rs, z_ss, z_rs, xa_ss, xa_rs, far,
):
    slab = lax.axis_index("slab")
    ctrl = lax.axis_index("ctrl")
    core = lax.rem(ctrl, 2)
    x = lax.rem(ctrl // 2, 4)
    z = ctrl // 8

    def at(z, x, core):
        return {"slab": slab, "ctrl": (z * 4 + x) * 2 + core}

    mates = [(lax.rem(x + dx, 4), lax.rem(core + dc, 2)) for dx, dc in OFFSETS]
    mate_ids = [at(z, mx, mc) for mx, mc in mates]
    z_peers = [at(lax.rem(z + k, 4), x, core) for k in (2, 1, 3)]
    below = {"slab": lax.rem(slab + 15, 16), "ctrl": ctrl}
    above = {"slab": lax.rem(slab + 1, 16), "ctrl": ctrl}
    peers = z_peers[1:] + [below, above] + mate_ids

    loads = [
        pltpu.make_async_copy(value, u.at[3 : 3 + NP, 8 : 8 + NY], load_sem.at[0]),
        pltpu.make_async_copy(speed, sp.at[2 : 2 + NP], load_sem.at[1]),
        pltpu.make_async_copy(reward, rw.at[:, 2 : 2 + NP], load_sem.at[2]),
        pltpu.make_async_copy(cset_in, cset, load_sem.at[3]),
        pltpu.make_async_copy(drift_in, drift, load_sem.at[4]),
        pltpu.make_async_copy(diff_in, diff, load_sem.at[5]),
    ]
    for load in loads:
        load.start()

    barrier = pltpu.get_barrier_semaphore()
    for peer in peers:
        pl.semaphore_signal(barrier, inc=1, device_id=peer, device_id_type=MESH)

    strip = jnp.zeros((8, NZ), F32)

    def clear(i, carry):
        u[i, 0:8] = strip
        u[i, 8 + NY : 16 + NY] = strip
        return carry

    lax.fori_loop(0, NP + 6, clear, 0)

    def clear_one(i, carry):
        for c in range(2):
            f1[c, i, 0:8] = strip
            f1[c, i, 8 + NY : 16 + NY] = strip
        return carry

    lax.fori_loop(0, NP + 4, clear_one, 0)

    def clear_two(i, carry):
        for c in range(2):
            f2[c, i, 0:8] = strip
            f2[c, i, 8 + NY : 16 + NY] = strip
        return carry

    lax.fori_loop(0, NP + 2, clear_two, 0)

    for load in loads[3:]:
        load.wait()
    a, e, pos_b, mid, total = [], [], [], [], []
    for c in range(2):
        k = cset[c]
        a.append([diff[d, k] for d in range(3)])
        b = [drift[d, k] for d in range(3)]
        e.append([jnp.abs(bd) for bd in b])
        pos_b.append(b)
        mid.append(1.0 - 2.0 * (a[c][0] + a[c][1] + a[c][2]))
        total.append(e[c][0] + e[c][1] + e[c][2])

    lane = lax.broadcasted_iota(jnp.int32, (BLK, NZ), 1)
    not_last = lane < NZ - 1
    not_first = lane > 0

    def neighbours(src, p, r0):
        here = src[p, 8 + r0 : 8 + r0 + BLK]
        ahead = [
            src[p + 1, 8 + r0 : 8 + r0 + BLK],
            src[p, 9 + r0 : 9 + r0 + BLK],
            jnp.where(not_last, pltpu.roll(here, NZ - 1, 1), 0.0),
        ]
        behind = [
            src[p - 1, 8 + r0 : 8 + r0 + BLK],
            src[p, 7 + r0 : 7 + r0 + BLK],
            jnp.where(not_first, pltpu.roll(here, 1, 1), 0.0),
        ]
        sums = [f + g for f, g in zip(ahead, behind)]
        return here, ahead, behind, sums

    def advance(step, p, r0):
        pace = sp[p + 2, r0 : r0 + BLK]
        if step == 0:
            shared = neighbours(u, p + 3, r0)
        results = []
        for c in range(2):
            if step == 0:
                here, ahead, behind, sums = shared
            elif step == 1:
                here, ahead, behind, sums = neighbours(f1.at[c], p + 2, r0)
            else:
                here, ahead, behind, sums = neighbours(f2.at[c], p + 1, r0)
            pay = rw[c, p + 2, r0 : r0 + BLK].astype(F32)
            wind = [
                e[c][d] * jnp.where(jnp.full((BLK, NZ), pos_b[c][d], F32) > 0.0, ahead[d], behind[d])
                for d in range(3)
            ]
            spread = (a[c][0] * sums[0] + a[c][1] * sums[1]) + (a[c][2] * sums[2] + mid[c] * here)
            flow = (wind[0] + wind[1]) + (wind[2] - total[c] * here)
            results.append((spread + pay) + pace * flow)
        return results

    def inside(p):
        lost = jnp.logical_or(jnp.logical_and(p < 0, slab == 0), jnp.logical_and(p >= NP, slab == 15))
        return jnp.where(lost, jnp.float32(0.0), jnp.float32(1.0))

    def sweep(step, low, high, o, part):
        def body(j, carry):
            if part == 0:
                p, pos = j, j - 6
            elif part == 1:
                p, pos = pair_plane(j, step + 1), j + 4
            else:
                p, pos = pair_plane(j, step - 2), j + 10
                keep = inside(p)
            for r0 in range(0, NY, BLK):
                both = advance(step, p, r0)
                if step < 2:
                    dst, off = (f1, 2) if step == 0 else (f2, 1)
                    for c in range(2):
                        dst[c, p + off, 8 + r0 : 8 + r0 + BLK] = both[c] * keep if part == 2 else both[c]
                else:
                    code = encode(jnp.maximum(both[0], both[1]))
                    for i in range(BLK // 16):
                        h, q = divmod(r0 // 16 + i, 4)
                        enc[o, h, q, pos] = code[16 * i : 16 * i + 16]
            return carry

        lax.fori_loop(low, high, body, 0)

    def remote(src, dst, ss, rs, peer):
        return pltpu.make_async_remote_copy(
            src_ref=src, dst_ref=dst, send_sem=ss, recv_sem=rs, device_id=peer, device_id_type=MESH
        )

    sent = []

    def start(copies):
        for copy in copies:
            copy.start()
            sent.append(copy)
        return copies

    def arrived(copies):
        for copy in copies:
            copy.wait_recv()

    flight = {}

    def each(ci, body):
        first, count = CHUNKS[ci]

        def step(i, carry):
            body(i)
            return carry

        lax.fori_loop(first, first + count, step, 0)

    def cut(ci):
        first, count = CHUNKS[ci]
        return slice(first, first + count)

    def send_max(o, ci):
        w = cut(ci)
        flight["x", o, ci] = start(
            [
                remote(enc.at[o, mc, mx, w], rx.at[o, k, w], x_ss.at[o, ci, k], x_rs.at[o, ci, k], mate_ids[k])
                for k, (mx, mc) in enumerate(mates)
            ]
        )

    def merge_x(o, ci):
        w = cut(ci)
        arrived(flight["x", o, ci])

        def body(i):
            hx[o, i] = top(enc[o, core, x, i], *[rx[o, k, i] for k in range(7)])

        each(ci, body)
        flight["z", o, ci] = start(
            [
                remote(hx.at[o, w], rz.at[o, k, w], z_ss.at[o, ci, k], z_rs.at[o, ci, k], z_peers[k])
                for k in range(3)
            ]
        )

    def merge_z(o, ci):
        w = cut(ci)
        arrived(flight["z", o, ci])

        def body(i):
            res[o, core, x, i] = top(hx[o, i], rz[o, 0, i], rz[o, 1, i], rz[o, 2, i])

        each(ci, body)
        mine = res.at[o, core, x, w]
        flight["xa", o, ci] = start(
            [remote(mine, mine, xa_ss.at[o, ci, k], xa_rs.at[o, ci, k], mate_ids[k]) for k in range(7)]
        )

    def finish(o, ci):
        arrived(flight["xa", o, ci])

        def body(i):
            if ci == 0:
                p = i + 6
            elif ci == 1:
                p = pair_plane(i - 4, 3)
            else:
                p = pair_plane(i - 10, 0)
            for h in range(2):
                for q in range(4):
                    row = 64 * h + 16 * q
                    if o == 0:
                        u[p + 3, 8 + row : 24 + row] = decode(res[o, h, q, i])
                    else:
                        out[p, row : row + 16] = res[o, h, q, i]

        each(ci, body)

    def send_low(o, low):
        flight["low", o] = start([remote(low, hv.at[o, 1], halo_ss.at[o, 0], halo_rs.at[o, 0], below)])

    def send_high(o, high):
        flight["high", o] = start([remote(high, hv.at[o, 0], halo_ss.at[o, 1], halo_rs.at[o, 1], above)])

    def take_halo(o):
        arrived(flight["low", o])
        arrived(flight["high", o])

        def body(i, carry):
            for side in range(2):
                p = i - 3 if side == 0 else i + NP
                keep = inside(p)
                for h in range(2):
                    for q in range(4):
                        row = 8 + 64 * h + 16 * q
                        u[p + 3, row : row + 16] = decode(hv[o, side, h, q, i]) * keep
            return carry

        lax.fori_loop(0, 3, body, 0)

    loads[0].wait()

    def stage(i, carry):
        for side in range(2):
            p = i if side == 0 else i + NP - 3
            for h in range(2):
                for q in range(4):
                    row = 8 + 64 * h + 16 * q
                    vst[side, h, q, i] = encode(u[p + 3, row : row + 16])
        return carry

    lax.fori_loop(0, 3, stage, 0)
    loads[1].wait()

    def stage_speed(i, carry):
        for side in range(2):
            p = i if side == 0 else i + NP - 2
            for r0 in range(0, NY, BLK):
                sst[side, i, r0 : r0 + BLK] = encode_speed(sp[p + 2, r0 : r0 + BLK])
        return carry

    lax.fori_loop(0, 2, stage_speed, 0)
    pl.semaphore_wait(barrier, len(peers))
    pl.semaphore_signal(far, inc=1, device_id=z_peers[1], device_id_type=MESH)
    send_low(0, vst.at[0])
    send_high(0, vst.at[1])
    extras = start(
        [
            remote(sst.at[0], hs.at[1], halo_ss.at[2, 0], halo_rs.at[2, 0], below),
            remote(sst.at[1], hs.at[0], halo_ss.at[2, 1], halo_rs.at[2, 1], above),
            remote(reward.at[:, 0:2], rw.at[:, NP + 2 : NP + 4], halo_ss.at[3, 0], halo_rs.at[3, 0], below),
            remote(reward.at[:, NP - 2 : NP], rw.at[:, 0:2], halo_ss.at[3, 1], halo_rs.at[3, 1], above),
        ]
    )
    loads[2].wait()

    def inner(o):
        for step in range(3):
            sweep(step, 4 + step, 12 - step, o, 0)
        send_max(o, 0)

    def middle(o):
        for step in range(3):
            sweep(step, 0, 6, o, 1)
        send_max(o, 1)

    def outer_face(o, side):
        for step in range(3):
            sweep(step, 3 * side, 3 * side + 3, o, 2)
        send_max(o, 2 + side)

    def take_speed(i, carry):
        for side in range(2):
            p = i - 2 if side == 0 else i + NP
            for r0 in range(0, NY, BLK):
                sp[p + 2, r0 : r0 + BLK] = decode_speed(hs[side, i, r0 : r0 + BLK])
        return carry

    inner(0)
    middle(0)
    pl.semaphore_wait(far, 1)
    merge_x(0, 0)
    take_halo(0)
    arrived(extras)
    lax.fori_loop(0, 2, take_speed, 0)
    outer_face(0, 0)
    merge_x(0, 1)
    outer_face(0, 1)
    merge_x(0, 2)
    merge_x(0, 3)
    merge_z(0, 0)
    merge_z(0, 1)
    merge_z(0, 2)
    merge_z(0, 3)
    finish(0, 0)
    finish(0, 1)

    inner(1)
    finish(0, 2)
    send_low(1, res.at[0, :, :, 10:13])
    finish(0, 3)
    send_high(1, res.at[0, :, :, 13:16])
    middle(1)
    merge_x(1, 0)
    take_halo(1)
    outer_face(1, 0)
    merge_x(1, 1)
    outer_face(1, 1)
    merge_x(1, 2)
    merge_x(1, 3)
    for ci in range(4):
        merge_z(1, ci)
    for ci in range(4):
        finish(1, ci)
    for copy in sent:
        copy.wait_send()


def body(value, speed, reward, ctrl_set, drift_sets, diffusion_sets):
    hbm = pl.BlockSpec(memory_space=pl.ANY)
    dma = pltpu.SemaphoreType.DMA
    n = len(CHUNKS)
    code = pl.pallas_call(
        kernel,
        out_shape=jax.ShapeDtypeStruct((NP, NY, NZ), I16),
        in_specs=[hbm] * 6,
        out_specs=pl.BlockSpec(memory_space=pltpu.VMEM),
        scratch_shapes=[
            pltpu.SMEM((2,), jnp.int32),
            pltpu.SMEM((3, 16), F32),
            pltpu.SMEM((3, 16), F32),
            pltpu.VMEM((NP + 6, NY + 16, NZ), F32),
            pltpu.VMEM((NP + 4, NY, NZ), F32),
            pltpu.VMEM((2, NP + 4, NY, NZ), jnp.bfloat16),
            pltpu.VMEM((2, NP + 4, NY + 16, NZ), F32),
            pltpu.VMEM((2, NP + 2, NY + 16, NZ), F32),
            pltpu.VMEM((2, 2, 4, NP, 16, NZ), I16),
            pltpu.VMEM((2, 7, NP, 16, NZ), I16),
            pltpu.VMEM((2, NP, 16, NZ), I16),
            pltpu.VMEM((2, 3, NP, 16, NZ), I16),
            pltpu.VMEM((2, 2, 4, NP, 16, NZ), I16),
            pltpu.VMEM((2, 2, 4, 3, 16, NZ), I16),
            pltpu.VMEM((2, 2, 2, 4, 3, 16, NZ), I16),
            pltpu.VMEM((2, 2, NY, NZ), I16),
            pltpu.VMEM((2, 2, NY, NZ), I16),
            dma((6,)),
            dma((4, 2)), dma((4, 2)),
            dma((2, n, 7)), dma((2, n, 7)),
            dma((2, n, 3)), dma((2, n, 3)),
            dma((2, n, 7)), dma((2, n, 7)),
            pltpu.SemaphoreType.REGULAR,
        ],
        compiler_params=pltpu.CompilerParams(collective_id=0, has_side_effects=True),
        name="hjb",
    )(ctrl_set, drift_sets.T, diffusion_sets.T, value, speed, reward)
    return decode(code)


def solution(mesh):
    in_specs = (
        P("slab", None, None),
        P("slab", None, None),
        P("ctrl", "slab", None, None),
        P("ctrl"),
        P(),
        P(),
    )
    out_specs = P("slab", None, None)
    return jax.shard_map(body, mesh=mesh, in_specs=in_specs, out_specs=out_specs, check_vma=False)
```

```python
import functools

import jax
import jax.numpy as jnp
from jax import lax
from jax.experimental import pallas as pl
from jax.experimental.pallas import tpu as pltpu
from jax.sharding import PartitionSpec as P

MESH = pl.DeviceIdType.MESH
F32 = jnp.float32
I16 = jnp.int16
OUTER = 2
NP = 16
NY = 128
NZ = 128
BLK = 32
KEY = 32767.0 / 11.45**0.25
SKEY = 32767.0 / 0.376
CHUNKS = ((0, 4), (4, 6), (10, 3), (13, 3))
OFFSETS = tuple((dx, dc) for dx in (2, 1, 3, 0) for dc in range(2) if dx or dc)


def encode(v):
    root = lax.rsqrt(lax.rsqrt(jnp.maximum(jnp.abs(v), 1e-30)))
    size = root * KEY + 0.5
    return jnp.where(v < 0.0, -size, size).astype(jnp.int32).astype(I16)


def decode(code):
    g = code.astype(jnp.int32).astype(F32) * (1.0 / KEY)
    return (g * jnp.abs(g)) * (g * g)


def encode_speed(s):
    t = (s - 0.625) * SKEY
    return jnp.where(t < 0.0, t - 0.5, t + 0.5).astype(jnp.int32).astype(I16)


def decode_speed(code):
    return code.astype(jnp.int32).astype(F32) * (1.0 / SKEY) + 0.625


def top(*codes):
    best = codes[0].astype(jnp.int32).astype(F32)
    for code in codes[1:]:
        best = jnp.maximum(best, code.astype(jnp.int32).astype(F32))
    return best.astype(jnp.int32).astype(I16)


def pair_plane(j, base):
    return j + base + (j // 3) * (10 - 2 * base)


def kernel(
    cset_in, drift_in, diff_in, value, speed, reward, out,
    cset, drift, diff, u, sp, rw, f1, f2, enc, rx, hx, rz, res, vst, hv, sst, hs,
    load_sem, halo_ss, halo_rs, x_ss, x_rs, z_ss, z_rs, xa_ss, xa_rs, far,
):
    slab = lax.axis_index("slab")
    ctrl = lax.axis_index("ctrl")
    core = lax.rem(ctrl, 2)
    x = lax.rem(ctrl // 2, 4)
    z = ctrl // 8

    def at(z, x, core):
        return {"slab": slab, "ctrl": (z * 4 + x) * 2 + core}

    mates = [(lax.rem(x + dx, 4), lax.rem(core + dc, 2)) for dx, dc in OFFSETS]
    mate_ids = [at(z, mx, mc) for mx, mc in mates]
    z_peers = [at(lax.rem(z + k, 4), x, core) for k in (2, 1, 3)]
    below = {"slab": lax.rem(slab + 15, 16), "ctrl": ctrl}
    above = {"slab": lax.rem(slab + 1, 16), "ctrl": ctrl}
    has_below = slab > 0
    has_above = slab < 15
    greeted = jnp.where(has_below, 1, 0) + jnp.where(has_above, 1, 0) + 9

    barrier = pltpu.get_barrier_semaphore()

    def greet(peer):
        pl.semaphore_signal(barrier, inc=1, device_id=peer, device_id_type=MESH)

    pl.when(has_below)(lambda: greet(below))
    pl.when(has_above)(lambda: greet(above))
    for peer in z_peers[1:] + mate_ids:
        greet(peer)

    loads = [
        pltpu.make_async_copy(value, u.at[3 : 3 + NP, 8 : 8 + NY], load_sem.at[0]),
        pltpu.make_async_copy(speed, sp.at[2 : 2 + NP], load_sem.at[1]),
        pltpu.make_async_copy(reward, rw.at[:, 2 : 2 + NP], load_sem.at[2]),
        pltpu.make_async_copy(cset_in, cset, load_sem.at[3]),
        pltpu.make_async_copy(drift_in, drift, load_sem.at[4]),
        pltpu.make_async_copy(diff_in, diff, load_sem.at[5]),
    ]
    for load in loads:
        load.start()

    strip = jnp.zeros((8, NZ), F32)

    def clear(i, carry):
        u[i, 0:8] = strip
        u[i, 8 + NY : 16 + NY] = strip
        return carry

    lax.fori_loop(0, NP + 6, clear, 0)

    def clear_one(i, carry):
        for c in range(2):
            f1[c, i, 0:8] = strip
            f1[c, i, 8 + NY : 16 + NY] = strip
        return carry

    lax.fori_loop(0, NP + 4, clear_one, 0)

    def clear_two(i, carry):
        for c in range(2):
            f2[c, i, 0:8] = strip
            f2[c, i, 8 + NY : 16 + NY] = strip
        return carry

    lax.fori_loop(0, NP + 2, clear_two, 0)

    for load in loads[3:]:
        load.wait()
    a, e, pos_b, mid, total = [], [], [], [], []
    for c in range(2):
        k = cset[c]
        a.append([diff[d, k] for d in range(3)])
        b = [drift[d, k] for d in range(3)]
        e.append([jnp.abs(bd) for bd in b])
        pos_b.append(b)
        mid.append(1.0 - 2.0 * (a[c][0] + a[c][1] + a[c][2]))
        total.append(e[c][0] + e[c][1] + e[c][2])

    lane = lax.broadcasted_iota(jnp.int32, (BLK, NZ), 1)
    not_last = lane < NZ - 1
    not_first = lane > 0

    def neighbours(src, p, r0):
        here = src[p, 8 + r0 : 8 + r0 + BLK]
        ahead = [
            src[p + 1, 8 + r0 : 8 + r0 + BLK],
            src[p, 9 + r0 : 9 + r0 + BLK],
            jnp.where(not_last, pltpu.roll(here, NZ - 1, 1), 0.0),
        ]
        behind = [
            src[p - 1, 8 + r0 : 8 + r0 + BLK],
            src[p, 7 + r0 : 7 + r0 + BLK],
            jnp.where(not_first, pltpu.roll(here, 1, 1), 0.0),
        ]
        sums = [f + g for f, g in zip(ahead, behind)]
        return here, ahead, behind, sums

    def advance(step, p, r0):
        pace = sp[p + 2, r0 : r0 + BLK]
        if step == 0:
            shared = neighbours(u, p + 3, r0)
        results = []
        for c in range(2):
            if step == 0:
                here, ahead, behind, sums = shared
            elif step == 1:
                here, ahead, behind, sums = neighbours(f1.at[c], p + 2, r0)
            else:
                here, ahead, behind, sums = neighbours(f2.at[c], p + 1, r0)
            pay = rw[c, p + 2, r0 : r0 + BLK].astype(F32)
            wind = [
                e[c][d] * jnp.where(jnp.full((BLK, NZ), pos_b[c][d], F32) > 0.0, ahead[d], behind[d])
                for d in range(3)
            ]
            spread = (a[c][0] * sums[0] + a[c][1] * sums[1]) + (a[c][2] * sums[2] + mid[c] * here)
            flow = (wind[0] + wind[1]) + (wind[2] - total[c] * here)
            results.append((spread + pay) + pace * flow)
        return results

    def inside(p):
        lost = jnp.logical_or(jnp.logical_and(p < 0, slab == 0), jnp.logical_and(p >= NP, slab == 15))
        return jnp.full((BLK, NZ), jnp.where(lost, 0, 1), jnp.int32) > 0

    def sweep(step, low, high, o, part):
        def body(j, carry):
            if part == 0:
                p, pos = j, j - 6
            elif part == 1:
                p, pos = pair_plane(j, step + 1), j + 4
            else:
                p, pos = pair_plane(j, step - 2), j + 10
                keep = inside(p)
            for r0 in range(0, NY, BLK):
                both = advance(step, p, r0)
                if step < 2:
                    dst, off = (f1, 2) if step == 0 else (f2, 1)
                    for c in range(2):
                        dst[c, p + off, 8 + r0 : 8 + r0 + BLK] = jnp.where(keep, both[c], 0.0) if part == 2 else both[c]
                else:
                    code = encode(jnp.maximum(both[0], both[1]))
                    for i in range(BLK // 16):
                        h, q = divmod(r0 // 16 + i, 4)
                        enc[o, h, q, pos] = code[16 * i : 16 * i + 16]
            return carry

        lax.fori_loop(low, high, body, 0)

    def remote(src, dst, ss, rs, peer):
        return pltpu.make_async_remote_copy(
            src_ref=src, dst_ref=dst, send_sem=ss, recv_sem=rs, device_id=peer, device_id_type=MESH
        )

    def take(like, rs):
        remote(like, like, rs, rs, mate_ids[0]).wait_recv()

    def left(like, ss):
        remote(like, like, ss, ss, mate_ids[0]).wait_send()

    def each(ci, body):
        first, count = CHUNKS[ci]

        def step(i, carry):
            body(i)
            return carry

        lax.fori_loop(first, first + count, step, 0)

    def cut(ci):
        first, count = CHUNKS[ci]
        return slice(first, first + count)

    def send_max(o, ci):
        w = cut(ci)
        for k, (mx, mc) in enumerate(mates):
            remote(enc.at[o, mc, mx, w], rx.at[o, k, w], x_ss.at[o], x_rs.at[o, ci], mate_ids[k]).start()

    def merge_x(o, ci):
        w = cut(ci)
        take(rx.at[o, :, w], x_rs.at[o, ci])

        def body(i):
            hx[o, i] = top(enc[o, core, x, i], *[rx[o, k, i] for k in range(7)])

        each(ci, body)
        for k in range(3):
            remote(hx.at[o, w], rz.at[o, k, w], z_ss.at[o], z_rs.at[o, ci], z_peers[k]).start()

    def merge_z(o, ci):
        w = cut(ci)
        take(rz.at[o, :, w], z_rs.at[o, ci])

        def body(i):
            res[o, core, x, i] = top(hx[o, i], rz[o, 0, i], rz[o, 1, i], rz[o, 2, i])

        each(ci, body)
        mine = res.at[o, core, x, w]
        for k in range(7):
            remote(mine, mine, xa_ss.at[o], xa_rs.at[o, ci], mate_ids[k]).start()

    def finish(o, ci):
        take(rx.at[o, :, cut(ci)], xa_rs.at[o, ci])

        def body(i):
            if ci == 0:
                p = i + 6
            elif ci == 1:
                p = pair_plane(i - 4, 3)
            else:
                p = pair_plane(i - 10, 0)
            for h in range(2):
                for q in range(4):
                    row = 64 * h + 16 * q
                    if o == 0:
                        u[p + 3, 8 + row : 24 + row] = decode(res[o, h, q, i])
                    else:
                        out[p, row : row + 16] = res[o, h, q, i]

        each(ci, body)

    def to_below(o):
        src = vst.at[0] if o == 0 else res.at[0, :, :, 10:13]
        moves = [(src, hv.at[o, 1])]
        if o == 0:
            moves += [(sst.at[0], hs.at[1]), (reward.at[:, 0:2], rw.at[:, NP + 2 : NP + 4])]
        return [remote(f, t, halo_ss.at[o, 0, i], halo_rs.at[o, 0, i], below) for i, (f, t) in enumerate(moves)]

    def to_above(o):
        src = vst.at[1] if o == 0 else res.at[0, :, :, 13:16]
        moves = [(src, hv.at[o, 0])]
        if o == 0:
            moves += [(sst.at[1], hs.at[0]), (reward.at[:, NP - 2 : NP], rw.at[:, 0:2])]
        return [remote(f, t, halo_ss.at[o, 1, i], halo_rs.at[o, 1, i], above) for i, (f, t) in enumerate(moves)]

    def start_all(copies):
        for copy in copies:
            copy.start()

    def send_low(o):
        pl.when(has_below)(lambda: start_all(to_below(o)))

    def send_high(o):
        pl.when(has_above)(lambda: start_all(to_above(o)))

    def take_halo(o, side):
        def wait():
            for copy in to_above(o) if side == 0 else to_below(o):
                copy.wait_recv()

        pl.when(has_below if side == 0 else has_above)(wait)

        def body(i, carry):
            p = i - 3 if side == 0 else i + NP
            keep = inside(p)
            for h in range(2):
                for q in range(4):
                    row = 8 + 64 * h + 16 * q
                    u[p + 3, row : row + 16] = jnp.where(keep[0:16], decode(hv[o, side, h, q, i]), 0.0)
            return carry

        lax.fori_loop(0, 3, body, 0)
        if o == 0:

            def pace(i, carry):
                p = i - 2 if side == 0 else i + NP
                for r0 in range(0, NY, BLK):
                    sp[p + 2, r0 : r0 + BLK] = decode_speed(hs[side, i, r0 : r0 + BLK])
                return carry

            lax.fori_loop(0, 2, pace, 0)

    loads[0].wait()

    def stage(i, carry):
        for side in range(2):
            p = i if side == 0 else i + NP - 3
            for h in range(2):
                for q in range(4):
                    row = 8 + 64 * h + 16 * q
                    vst[side, h, q, i] = encode(u[p + 3, row : row + 16])
        return carry

    lax.fori_loop(0, 3, stage, 0)
    loads[1].wait()

    def stage_speed(i, carry):
        for side in range(2):
            p = i if side == 0 else i + NP - 2
            for r0 in range(0, NY, BLK):
                sst[side, i, r0 : r0 + BLK] = encode_speed(sp[p + 2, r0 : r0 + BLK])
        return carry

    lax.fori_loop(0, 2, stage_speed, 0)
    pl.semaphore_wait(barrier, greeted)
    pl.semaphore_signal(far, inc=1, device_id=z_peers[1], device_id_type=MESH)
    send_low(0)
    send_high(0)
    loads[2].wait()

    def inner(o):
        for step in range(3):
            sweep(step, 4 + step, 12 - step, o, 0)
        send_max(o, 0)

    def middle(o):
        for step in range(3):
            sweep(step, 0, 6, o, 1)
        send_max(o, 1)

    def outer_face(o, side):
        for step in range(3):
            sweep(step, 3 * side, 3 * side + 3, o, 2)
        send_max(o, 2 + side)

    inner(0)
    middle(0)
    pl.semaphore_wait(far, 1)
    merge_x(0, 0)
    take_halo(0, 0)
    outer_face(0, 0)
    merge_x(0, 1)
    take_halo(0, 1)
    outer_face(0, 1)
    merge_x(0, 2)
    merge_x(0, 3)
    for ci in range(4):
        merge_z(0, ci)
    finish(0, 0)
    finish(0, 1)

    for step in range(2):
        sweep(step, 4 + step, 12 - step, 1, 0)
    finish(0, 2)
    send_low(1)
    sweep(2, 6, 10, 1, 0)
    send_max(1, 0)
    finish(0, 3)
    send_high(1)
    middle(1)
    merge_x(1, 0)
    take_halo(1, 1)
    outer_face(1, 1)
    take_halo(1, 0)
    outer_face(1, 0)
    order = (0, 1, 3, 2)
    for ci in order[1:]:
        merge_x(1, ci)
    for ci in order:
        merge_z(1, ci)
    for ci in order:
        finish(1, ci)

    for o in range(2):
        left(rx.at[o], x_ss.at[o])
        left(rz.at[o], z_ss.at[o])
        left(rx.at[o], xa_ss.at[o])

        def low_left():
            for copy in to_below(o):
                copy.wait_send()

        def high_left():
            for copy in to_above(o):
                copy.wait_send()

        pl.when(has_below)(low_left)
        pl.when(has_above)(high_left)


def body(value, speed, reward, ctrl_set, drift_sets, diffusion_sets):
    hbm = pl.BlockSpec(memory_space=pl.ANY)
    dma = pltpu.SemaphoreType.DMA
    n = len(CHUNKS)
    code = pl.pallas_call(
        kernel,
        out_shape=pltpu.VMEM((NP, NY, NZ), I16),
        in_specs=[hbm] * 6,
        out_specs=pl.BlockSpec(memory_space=pltpu.VMEM),
        scratch_shapes=[
            pltpu.SMEM((2,), jnp.int32),
            pltpu.SMEM((3, 16), F32),
            pltpu.SMEM((3, 16), F32),
            pltpu.VMEM((NP + 6, NY + 16, NZ), F32),
            pltpu.VMEM((NP + 4, NY, NZ), F32),
            pltpu.VMEM((2, NP + 4, NY, NZ), jnp.bfloat16),
            pltpu.VMEM((2, NP + 4, NY + 16, NZ), F32),
            pltpu.VMEM((2, NP + 2, NY + 16, NZ), F32),
            pltpu.VMEM((2, 2, 4, NP, 16, NZ), I16),
            pltpu.VMEM((2, 7, NP, 16, NZ), I16),
            pltpu.VMEM((2, NP, 16, NZ), I16),
            pltpu.VMEM((2, 3, NP, 16, NZ), I16),
            pltpu.VMEM((2, 2, 4, NP, 16, NZ), I16),
            pltpu.VMEM((2, 2, 4, 3, 16, NZ), I16),
            pltpu.VMEM((2, 2, 2, 4, 3, 16, NZ), I16),
            pltpu.VMEM((2, 2, NY, NZ), I16),
            pltpu.VMEM((2, 2, NY, NZ), I16),
            dma((6,)),
            dma((2, 2, 3)), dma((2, 2, 3)),
            dma((2,)), dma((2, n)),
            dma((2,)), dma((2, n)),
            dma((2,)), dma((2, n)),
            pltpu.SemaphoreType.REGULAR,
        ],
        compiler_params=pltpu.CompilerParams(collective_id=0, has_side_effects=True),
        name="hjb",
    )(ctrl_set, drift_sets.T, diffusion_sets.T, value, speed, reward)
    return decode(code)


def solution(mesh):
    in_specs = (
        P("slab", None, None),
        P("slab", None, None),
        P("ctrl", "slab", None, None),
        P("ctrl"),
        P(),
        P(),
    )
    out_specs = P("slab", None, None)
    return jax.shard_map(body, mesh=mesh, in_specs=in_specs, out_specs=out_specs, check_vma=False)
```

```python
import functools

import jax
import jax.numpy as jnp
from jax import lax
from jax.experimental import pallas as pl
from jax.experimental.pallas import tpu as pltpu
from jax.sharding import PartitionSpec as P

MESH = pl.DeviceIdType.MESH
F32 = jnp.float32
I16 = jnp.int16
OUTER = 2
NP = 16
NY = 128
NZ = 128
BLK = 32
KEY = 32767.0 / 11.45**0.25
SKEY = 32767.0 / 0.376
CHUNKS = ((0, 4), (4, 3), (7, 3), (10, 3), (13, 3))
OFFSETS = tuple((dx, dc) for dx in (2, 1, 3, 0) for dc in range(2) if dx or dc)


def encode(v):
    root = lax.rsqrt(lax.rsqrt(jnp.maximum(jnp.abs(v), 1e-30)))
    size = root * KEY + 0.5
    return jnp.where(v < 0.0, -size, size).astype(jnp.int32).astype(I16)


def decode(code):
    g = code.astype(jnp.int32).astype(F32) * (1.0 / KEY)
    return (g * jnp.abs(g)) * (g * g)


def encode_speed(s):
    t = (s - 0.625) * SKEY
    return jnp.where(t < 0.0, t - 0.5, t + 0.5).astype(jnp.int32).astype(I16)


def decode_speed(code):
    return code.astype(jnp.int32).astype(F32) * (1.0 / SKEY) + 0.625


def top(*codes):
    best = codes[0].astype(jnp.int32).astype(F32)
    for code in codes[1:]:
        best = jnp.maximum(best, code.astype(jnp.int32).astype(F32))
    return best.astype(jnp.int32).astype(I16)


def pair_plane(j, base):
    return j + base + (j // 3) * (10 - 2 * base)


def kernel(
    cset_in, drift_in, diff_in, value, speed, reward, out,
    cset, drift, diff, u, sp, rw, wide, f1, f2, enc, rx, hx, rz, res, vst, hv, sst, hs,
    load_sem, halo_ss, halo_rs, pass_ss, pass_rs, x_ss, x_rs, z_ss, z_rs, xa_ss, xa_rs, far,
):
    slab = lax.axis_index("slab")
    ctrl = lax.axis_index("ctrl")
    core = lax.rem(ctrl, 2)
    x = lax.rem(ctrl // 2, 4)
    z = ctrl // 8

    def at(z, x, core):
        return {"slab": slab, "ctrl": (z * 4 + x) * 2 + core}

    mates = [(lax.rem(x + dx, 4), lax.rem(core + dc, 2)) for dx, dc in OFFSETS]
    mate_ids = [at(z, mx, mc) for mx, mc in mates]
    z_peers = [at(lax.rem(z + k, 4), x, core) for k in (2, 1, 3)]
    below = {"slab": lax.rem(slab + 15, 16), "ctrl": ctrl}
    above = {"slab": lax.rem(slab + 1, 16), "ctrl": ctrl}
    has_below = slab > 0
    has_above = slab < 15
    greeted = jnp.where(has_below, 1, 0) + jnp.where(has_above, 1, 0) + 9

    barrier = pltpu.get_barrier_semaphore()

    def greet(peer):
        pl.semaphore_signal(barrier, inc=1, device_id=peer, device_id_type=MESH)

    pl.when(has_below)(lambda: greet(below))
    pl.when(has_above)(lambda: greet(above))
    for peer in z_peers[1:] + mate_ids:
        greet(peer)

    loads = [
        pltpu.make_async_copy(value, u.at[3 : 3 + NP, 8 : 8 + NY], load_sem.at[0]),
        pltpu.make_async_copy(speed, sp.at[2 : 2 + NP], load_sem.at[1]),
        pltpu.make_async_copy(reward, rw.at[:, 2 : 2 + NP], load_sem.at[2]),
        pltpu.make_async_copy(cset_in, cset, load_sem.at[3]),
        pltpu.make_async_copy(drift_in, drift, load_sem.at[4]),
        pltpu.make_async_copy(diff_in, diff, load_sem.at[5]),
    ]
    for load in loads:
        load.start()

    strip = jnp.zeros((8, NZ), F32)

    def clear(i, carry):
        u[i, 0:8] = strip
        u[i, 8 + NY : 16 + NY] = strip
        return carry

    lax.fori_loop(0, NP + 6, clear, 0)

    def clear_one(i, carry):
        for c in range(2):
            f1[c, i, 0:8] = strip
            f1[c, i, 8 + NY : 16 + NY] = strip
        return carry

    lax.fori_loop(0, NP + 4, clear_one, 0)

    def clear_two(i, carry):
        for c in range(2):
            f2[c, i, 0:8] = strip
            f2[c, i, 8 + NY : 16 + NY] = strip
        return carry

    lax.fori_loop(0, NP + 2, clear_two, 0)

    for load in loads[3:]:
        load.wait()
    a, e, pos_b, mid, total = [], [], [], [], []
    for c in range(2):
        k = cset[c]
        a.append([diff[d, k] for d in range(3)])
        b = [drift[d, k] for d in range(3)]
        e.append([jnp.abs(bd) for bd in b])
        pos_b.append(b)
        mid.append(1.0 - 2.0 * (a[c][0] + a[c][1] + a[c][2]))
        total.append(e[c][0] + e[c][1] + e[c][2])

    lane = lax.broadcasted_iota(jnp.int32, (BLK, NZ), 1)
    not_last = lane < NZ - 1
    not_first = lane > 0

    def neighbours(src, p, r0):
        here = src[p, 8 + r0 : 8 + r0 + BLK]
        ahead = [
            src[p + 1, 8 + r0 : 8 + r0 + BLK],
            src[p, 9 + r0 : 9 + r0 + BLK],
            jnp.where(not_last, pltpu.roll(here, NZ - 1, 1), 0.0),
        ]
        behind = [
            src[p - 1, 8 + r0 : 8 + r0 + BLK],
            src[p, 7 + r0 : 7 + r0 + BLK],
            jnp.where(not_first, pltpu.roll(here, 1, 1), 0.0),
        ]
        sums = [f + g for f, g in zip(ahead, behind)]
        return here, ahead, behind, sums

    def advance(step, p, r0, o):
        pace = sp[p + 2, r0 : r0 + BLK]
        if step == 0:
            shared = neighbours(u, p + 3, r0)
        results = []
        for c in range(2):
            if step == 0:
                here, ahead, behind, sums = shared
            elif step == 1:
                here, ahead, behind, sums = neighbours(f1.at[c], p + 2, r0)
            else:
                here, ahead, behind, sums = neighbours(f2.at[c], p + 1, r0)
            if step == 0 and o == 0:
                pay = rw[c, p + 2, r0 : r0 + BLK].astype(F32)
                wide[c, p + 2, r0 : r0 + BLK] = pay
            else:
                pay = wide[c, p + 2, r0 : r0 + BLK]
            wind = [
                e[c][d] * jnp.where(jnp.full((BLK, NZ), pos_b[c][d], F32) > 0.0, ahead[d], behind[d])
                for d in range(3)
            ]
            spread = (a[c][0] * sums[0] + a[c][1] * sums[1]) + (a[c][2] * sums[2] + mid[c] * here)
            flow = (wind[0] + wind[1]) + (wind[2] - total[c] * here)
            results.append((spread + pay) + pace * flow)
        return results

    def inside(p):
        lost = jnp.logical_or(jnp.logical_and(p < 0, slab == 0), jnp.logical_and(p >= NP, slab == 15))
        return jnp.full((BLK, NZ), jnp.where(lost, 0, 1), jnp.int32) > 0

    def sweep(step, low, high, o, part):
        def body(j, carry):
            if part == 0:
                p, pos = j, j - 6
            elif part == 1:
                p, pos = pair_plane(j, step + 1), j + 4
            else:
                p, pos = pair_plane(j, step - 2), j + 10
                keep = inside(p)
            for r0 in range(0, NY, BLK):
                both = advance(step, p, r0, o)
                if step < 2:
                    dst, off = (f1, 2) if step == 0 else (f2, 1)
                    for c in range(2):
                        dst[c, p + off, 8 + r0 : 8 + r0 + BLK] = jnp.where(keep, both[c], 0.0) if part == 2 else both[c]
                else:
                    code = encode(jnp.maximum(both[0], both[1]))
                    for i in range(BLK // 16):
                        h, q = divmod(r0 // 16 + i, 4)
                        enc[o, h, q, pos] = code[16 * i : 16 * i + 16]
            return carry

        lax.fori_loop(low, high, body, 0, unroll=3 if part else 2)

    def remote(src, dst, ss, rs, peer):
        return pltpu.make_async_remote_copy(
            src_ref=src, dst_ref=dst, send_sem=ss, recv_sem=rs, device_id=peer, device_id_type=MESH
        )

    def take(like, rs):
        remote(like, like, rs, rs, mate_ids[0]).wait_recv()

    def left(like, ss):
        remote(like, like, ss, ss, mate_ids[0]).wait_send()

    def each(ci, body):
        first, count = CHUNKS[ci]

        def step(i, carry):
            body(i)
            return carry

        lax.fori_loop(first, first + count, step, 0)

    def cut(ci):
        first, count = CHUNKS[ci]
        return slice(first, first + count)

    def send_max(o, ci):
        w = cut(ci)
        for k, (mx, mc) in enumerate(mates):
            remote(enc.at[o, mc, mx, w], rx.at[o, k, w], x_ss.at[o], x_rs.at[o, ci], mate_ids[k]).start()

    def merge_x(o, ci):
        w = cut(ci)
        take(rx.at[o, :, w], x_rs.at[o, ci])

        def body(i):
            hx[o, i] = top(enc[o, core, x, i], *[rx[o, k, i] for k in range(7)])

        each(ci, body)
        for k in range(3):
            remote(hx.at[o, w], rz.at[o, k, w], z_ss.at[o], z_rs.at[o, ci], z_peers[k]).start()

    def merge_z(o, ci):
        w = cut(ci)
        take(rz.at[o, :, w], z_rs.at[o, ci])

        def body(i):
            res[o, core, x, i] = top(hx[o, i], rz[o, 0, i], rz[o, 1, i], rz[o, 2, i])

        each(ci, body)
        mine = res.at[o, core, x, w]
        for k in range(7):
            remote(mine, mine, xa_ss.at[o], xa_rs.at[o, ci], mate_ids[k]).start()

    def finish(o, ci):
        take(rx.at[o, :, cut(ci)], xa_rs.at[o, ci])

        def body(i):
            if ci == 0:
                p = i + 6
            elif ci < 3:
                p = pair_plane(i - 4, 3)
            else:
                p = pair_plane(i - 10, 0)
            for h in range(2):
                for q in range(4):
                    row = 64 * h + 16 * q
                    if o == 0:
                        u[p + 3, 8 + row : 24 + row] = decode(res[o, h, q, i])
                    else:
                        out[p, row : row + 16] = res[o, h, q, i]

        each(ci, body)

    def to_below(o):
        if o == 0:
            moves = [
                (vst.at[0, core], hv.at[0, 1, core]),
                (sst.at[0, core], hs.at[1, core]),
                (reward.at[:, 0:2], rw.at[:, NP + 2 : NP + 4]),
            ]
        else:
            moves = [(res.at[0, :, :, 10:13], hv.at[1, 1])]
        return [remote(f, t, halo_ss.at[o, 0, i], halo_rs.at[o, 0, i], below) for i, (f, t) in enumerate(moves)]

    def to_above(o):
        if o == 0:
            moves = [
                (vst.at[1, core], hv.at[0, 0, core]),
                (sst.at[1, core], hs.at[0, core]),
                (reward.at[:, NP - 2 : NP], rw.at[:, 0:2]),
            ]
        else:
            moves = [(res.at[0, :, :, 13:16], hv.at[1, 0])]
        return [remote(f, t, halo_ss.at[o, 1, i], halo_rs.at[o, 1, i], above) for i, (f, t) in enumerate(moves)]

    def to_mate(side):
        moves = [(hv.at[0, side, core], hv.at[0, side, core]), (hs.at[side, core], hs.at[side, core])]
        return [remote(f, t, pass_ss.at[side, i], pass_rs.at[side, i], mate_ids[-1]) for i, (f, t) in enumerate(moves)]

    def pass_on(side):
        def go():
            halves = to_above(0) if side == 0 else to_below(0)
            for half, copy in zip(halves, to_mate(side)):
                half.wait_recv()
                copy.start()

        pl.when(has_below if side == 0 else has_above)(go)

    def start_all(copies):
        for copy in copies:
            copy.start()

    def send_low(o):
        pl.when(has_below)(lambda: start_all(to_below(o)))

    def send_high(o):
        pl.when(has_above)(lambda: start_all(to_above(o)))

    def take_halo(o, side):
        def wait():
            copies = to_above(o) if side == 0 else to_below(o)
            if o == 0:
                copies = to_mate(side) + copies[2:]
            for copy in copies:
                copy.wait_recv()

        pl.when(has_below if side == 0 else has_above)(wait)

        def body(i, carry):
            p = i - 3 if side == 0 else i + NP
            keep = inside(p)
            for h in range(2):
                for q in range(4):
                    row = 8 + 64 * h + 16 * q
                    u[p + 3, row : row + 16] = jnp.where(keep[0:16], decode(hv[o, side, h, q, i]), 0.0)
            return carry

        lax.fori_loop(0, 3, body, 0)
        if o == 0:

            def pace(i, carry):
                p = i - 2 if side == 0 else i + NP
                for r0 in range(0, NY, BLK):
                    sp[p + 2, r0 : r0 + BLK] = decode_speed(hs[side, r0 // 64, i, r0 % 64 : r0 % 64 + BLK])
                return carry

            lax.fori_loop(0, 2, pace, 0)

    loads[0].wait()

    def stage(i, carry):
        for side in range(2):
            p = i if side == 0 else i + NP - 3
            for h in range(2):
                for q in range(4):
                    row = 8 + 64 * h + 16 * q
                    vst[side, h, q, i] = encode(u[p + 3, row : row + 16])
        return carry

    lax.fori_loop(0, 3, stage, 0)
    loads[1].wait()

    def stage_speed(i, carry):
        for side in range(2):
            p = i if side == 0 else i + NP - 2
            for r0 in range(0, NY, BLK):
                sst[side, r0 // 64, i, r0 % 64 : r0 % 64 + BLK] = encode_speed(sp[p + 2, r0 : r0 + BLK])
        return carry

    lax.fori_loop(0, 2, stage_speed, 0)
    pl.semaphore_wait(barrier, greeted)
    pl.semaphore_signal(far, inc=1, device_id=z_peers[1], device_id_type=MESH)
    send_low(0)
    send_high(0)
    loads[2].wait()

    def inner(o):
        for step in range(3):
            sweep(step, 4 + step, 12 - step, o, 0)
        send_max(o, 0)

    def middle(o, side):
        for step in range(3):
            sweep(step, 3 * side, 3 * side + 3, o, 1)
        send_max(o, 1 + side)

    def face(o, side):
        take_halo(o, side)
        for step in range(3):
            sweep(step, 3 * side, 3 * side + 3, o, 2)
        send_max(o, 3 + side)

    inner(0)
    middle(0, 0)
    middle(0, 1)
    pl.semaphore_wait(far, 1)
    pass_on(0)
    pass_on(1)
    merge_x(0, 0)
    face(0, 0)
    merge_x(0, 1)
    face(0, 1)
    for ci in (2, 3, 4):
        merge_x(0, ci)
    for ci in range(5):
        merge_z(0, ci)
    for ci in range(3):
        finish(0, ci)

    for step in range(2):
        sweep(step, 4 + step, 12 - step, 1, 0)
    finish(0, 3)
    send_low(1)
    sweep(2, 6, 10, 1, 0)
    send_max(1, 0)
    middle(1, 0)
    finish(0, 4)
    send_high(1)
    middle(1, 1)
    merge_x(1, 0)
    face(1, 1)
    merge_x(1, 1)
    face(1, 0)
    order = (0, 1, 2, 4, 3)
    for ci in order[2:]:
        merge_x(1, ci)
    for ci in order:
        merge_z(1, ci)
    for ci in order:
        finish(1, ci)

    for o in range(2):
        left(rx.at[o], x_ss.at[o])
        left(rz.at[o], z_ss.at[o])
        left(rx.at[o], xa_ss.at[o])

        def low_left():
            for copy in to_below(o) + (to_mate(0) if o == 0 else []):
                copy.wait_send()

        def high_left():
            for copy in to_above(o) + (to_mate(1) if o == 0 else []):
                copy.wait_send()

        pl.when(has_below)(low_left)
        pl.when(has_above)(high_left)


def body(value, speed, reward, ctrl_set, drift_sets, diffusion_sets):
    hbm = pl.BlockSpec(memory_space=pl.ANY)
    dma = pltpu.SemaphoreType.DMA
    n = len(CHUNKS)
    code = pl.pallas_call(
        kernel,
        out_shape=pltpu.VMEM((NP, NY, NZ), I16),
        in_specs=[hbm] * 6,
        out_specs=pl.BlockSpec(memory_space=pltpu.VMEM),
        scratch_shapes=[
            pltpu.SMEM((2,), jnp.int32),
            pltpu.SMEM((3, 16), F32),
            pltpu.SMEM((3, 16), F32),
            pltpu.VMEM((NP + 6, NY + 16, NZ), F32),
            pltpu.VMEM((NP + 4, NY, NZ), F32),
            pltpu.VMEM((2, NP + 4, NY, NZ), jnp.bfloat16),
            pltpu.VMEM((2, NP + 4, NY, NZ), F32),
            pltpu.VMEM((2, NP + 4, NY + 16, NZ), F32),
            pltpu.VMEM((2, NP + 2, NY + 16, NZ), F32),
            pltpu.VMEM((2, 2, 4, NP, 16, NZ), I16),
            pltpu.VMEM((2, 7, NP, 16, NZ), I16),
            pltpu.VMEM((2, NP, 16, NZ), I16),
            pltpu.VMEM((2, 3, NP, 16, NZ), I16),
            pltpu.VMEM((2, 2, 4, NP, 16, NZ), I16),
            pltpu.VMEM((2, 2, 4, 3, 16, NZ), I16),
            pltpu.VMEM((2, 2, 2, 4, 3, 16, NZ), I16),
            pltpu.VMEM((2, 2, 2, NY // 2, NZ), I16),
            pltpu.VMEM((2, 2, 2, NY // 2, NZ), I16),
            dma((6,)),
            dma((2, 2, 3)), dma((2, 2, 3)),
            dma((2, 2)), dma((2, 2)),
            dma((2,)), dma((2, n)),
            dma((2,)), dma((2, n)),
            dma((2,)), dma((2, n)),
            pltpu.SemaphoreType.REGULAR,
        ],
        compiler_params=pltpu.CompilerParams(collective_id=0, has_side_effects=True),
        name="hjb",
    )(ctrl_set, drift_sets.T, diffusion_sets.T, value, speed, reward)
    return decode(code)


def solution(mesh):
    in_specs = (
        P("slab", None, None),
        P("slab", None, None),
        P("ctrl", "slab", None, None),
        P("ctrl"),
        P(),
        P(),
    )
    out_specs = P("slab", None, None)
    return jax.shard_map(body, mesh=mesh, in_specs=in_specs, out_specs=out_specs, check_vma=False)
```

```python
import functools

import jax
import jax.numpy as jnp
from jax import lax
from jax.experimental import pallas as pl
from jax.experimental.pallas import tpu as pltpu
from jax.sharding import PartitionSpec as P

MESH = pl.DeviceIdType.MESH
F32 = jnp.float32
I16 = jnp.int16
OUTER = 2
NP = 16
NY = 128
NZ = 128
BLK = 32
KEY = 32767.0 / 11.45**0.25
SKEY = 32767.0 / 0.376
CHUNKS = ((0, 4), (4, 3), (7, 3), (10, 3), (13, 3))
OFFSETS = tuple((dx, dc) for dx in (2, 1, 3, 0) for dc in range(2) if dx or dc)


def encode(v):
    root = lax.rsqrt(lax.rsqrt(jnp.maximum(jnp.abs(v), 1e-30)))
    size = root * KEY + 0.5
    return jnp.where(v < 0.0, -size, size).astype(jnp.int32).astype(I16)


def decode(code):
    g = code.astype(jnp.int32).astype(F32) * (1.0 / KEY)
    return (g * jnp.abs(g)) * (g * g)


def encode_speed(s):
    t = (s - 0.625) * SKEY
    return jnp.where(t < 0.0, t - 0.5, t + 0.5).astype(jnp.int32).astype(I16)


def decode_speed(code):
    return code.astype(jnp.int32).astype(F32) * (1.0 / SKEY) + 0.625


def top(*codes):
    best = codes[0].astype(jnp.int32).astype(F32)
    for code in codes[1:]:
        best = jnp.maximum(best, code.astype(jnp.int32).astype(F32))
    return best.astype(jnp.int32).astype(I16)


def pair_plane(j, base):
    return j + base + (j // 3) * (10 - 2 * base)


def kernel(
    cset_in, drift_in, diff_in, value, speed, reward, out,
    cset, drift, diff, u, sp, rw, wide, f1, f2, enc, rx, hx, rz, res, vst, hv, sst, hs,
    load_sem, halo_ss, halo_rs, pass_ss, pass_rs, x_ss, x_rs, z_ss, z_rs, xa_ss, xa_rs, far,
):
    slab = lax.axis_index("slab")
    ctrl = lax.axis_index("ctrl")
    core = lax.rem(ctrl, 2)
    x = lax.rem(ctrl // 2, 4)
    z = ctrl // 8

    def at(z, x, core):
        return {"slab": slab, "ctrl": (z * 4 + x) * 2 + core}

    mates = [(lax.rem(x + dx, 4), lax.rem(core + dc, 2)) for dx, dc in OFFSETS]
    mate_ids = [at(z, mx, mc) for mx, mc in mates]
    z_peers = [at(lax.rem(z + k, 4), x, core) for k in (2, 1, 3)]
    below = {"slab": lax.rem(slab + 15, 16), "ctrl": ctrl}
    above = {"slab": lax.rem(slab + 1, 16), "ctrl": ctrl}
    has_below = slab > 0
    has_above = slab < 15
    greeted = jnp.where(has_below, 1, 0) + jnp.where(has_above, 1, 0) + 9

    def group(slab_id):
        ids = [ctrl] + [(z * 4 + mx) * 2 + mc for mx, mc in mates]
        return [{"slab": slab_id, "ctrl": i} for i in ids]


    barrier = pltpu.get_barrier_semaphore()

    def greet(peer):
        pl.semaphore_signal(barrier, inc=1, device_id=peer, device_id_type=MESH)

    pl.when(has_below)(lambda: greet(below))
    pl.when(has_above)(lambda: greet(above))
    for peer in z_peers[1:] + mate_ids:
        greet(peer)

    loads = [
        pltpu.make_async_copy(value, u.at[3 : 3 + NP, 8 : 8 + NY], load_sem.at[0]),
        pltpu.make_async_copy(speed, sp.at[2 : 2 + NP], load_sem.at[1]),
        pltpu.make_async_copy(reward, rw.at[:, 2 : 2 + NP], load_sem.at[2]),
        pltpu.make_async_copy(cset_in, cset, load_sem.at[3]),
        pltpu.make_async_copy(drift_in, drift, load_sem.at[4]),
        pltpu.make_async_copy(diff_in, diff, load_sem.at[5]),
    ]
    for load in loads:
        load.start()

    strip = jnp.zeros((8, NZ), F32)

    def clear(i, carry):
        u[i, 0:8] = strip
        u[i, 8 + NY : 16 + NY] = strip
        return carry

    lax.fori_loop(0, NP + 6, clear, 0)

    def clear_one(i, carry):
        for c in range(2):
            f1[c, i, 0:8] = strip
            f1[c, i, 8 + NY : 16 + NY] = strip
        return carry

    lax.fori_loop(0, NP + 4, clear_one, 0)

    def clear_two(i, carry):
        for c in range(2):
            f2[c, i, 0:8] = strip
            f2[c, i, 8 + NY : 16 + NY] = strip
        return carry

    lax.fori_loop(0, NP + 2, clear_two, 0)

    for load in loads[3:]:
        load.wait()
    a, e, pos_b, mid, total = [], [], [], [], []
    for c in range(2):
        k = cset[c]
        a.append([diff[d, k] for d in range(3)])
        b = [drift[d, k] for d in range(3)]
        e.append([jnp.abs(bd) for bd in b])
        pos_b.append(b)
        mid.append(1.0 - 2.0 * (a[c][0] + a[c][1] + a[c][2]))
        total.append(e[c][0] + e[c][1] + e[c][2])

    lane = lax.broadcasted_iota(jnp.int32, (BLK, NZ), 1)
    not_last = lane < NZ - 1
    not_first = lane > 0

    def neighbours(src, p, r0):
        here = src[p, 8 + r0 : 8 + r0 + BLK]
        ahead = [
            src[p + 1, 8 + r0 : 8 + r0 + BLK],
            src[p, 9 + r0 : 9 + r0 + BLK],
            jnp.where(not_last, pltpu.roll(here, NZ - 1, 1), 0.0),
        ]
        behind = [
            src[p - 1, 8 + r0 : 8 + r0 + BLK],
            src[p, 7 + r0 : 7 + r0 + BLK],
            jnp.where(not_first, pltpu.roll(here, 1, 1), 0.0),
        ]
        sums = [f + g for f, g in zip(ahead, behind)]
        return here, ahead, behind, sums

    def advance(step, p, r0, o):
        pace = sp[p + 2, r0 : r0 + BLK]
        if step == 0:
            shared = neighbours(u, p + 3, r0)
        results = []
        for c in range(2):
            if step == 0:
                here, ahead, behind, sums = shared
            elif step == 1:
                here, ahead, behind, sums = neighbours(f1.at[c], p + 2, r0)
            else:
                here, ahead, behind, sums = neighbours(f2.at[c], p + 1, r0)
            if step == 0 and o == 0:
                pay = rw[c, p + 2, r0 : r0 + BLK].astype(F32)
                wide[c, p + 2, r0 : r0 + BLK] = pay
            else:
                pay = wide[c, p + 2, r0 : r0 + BLK]
            wind = [
                e[c][d] * jnp.where(jnp.full((BLK, NZ), pos_b[c][d], F32) > 0.0, ahead[d], behind[d])
                for d in range(3)
            ]
            spread = (a[c][0] * sums[0] + a[c][1] * sums[1]) + (a[c][2] * sums[2] + mid[c] * here)
            flow = (wind[0] + wind[1]) + (wind[2] - total[c] * here)
            results.append((spread + pay) + pace * flow)
        return results

    def inside(p):
        lost = jnp.logical_or(jnp.logical_and(p < 0, slab == 0), jnp.logical_and(p >= NP, slab == 15))
        return jnp.full((BLK, NZ), jnp.where(lost, 0, 1), jnp.int32) > 0

    def sweep(step, low, high, o, part):
        def body(j, carry):
            if part == 0:
                p, pos = j, j - 6
            elif part == 1:
                p, pos = pair_plane(j, step + 1), j + 4
            else:
                p, pos = pair_plane(j, step - 2), j + 10
                keep = inside(p)
            for r0 in range(0, NY, BLK):
                both = advance(step, p, r0, o)
                if step < 2:
                    dst, off = (f1, 2) if step == 0 else (f2, 1)
                    for c in range(2):
                        dst[c, p + off, 8 + r0 : 8 + r0 + BLK] = jnp.where(keep, both[c], 0.0) if part == 2 else both[c]
                else:
                    code = encode(jnp.maximum(both[0], both[1]))
                    for i in range(BLK // 16):
                        h, q = divmod(r0 // 16 + i, 4)
                        enc[o, h, q, pos] = code[16 * i : 16 * i + 16]
            return carry

        lax.fori_loop(low, high, body, 0, unroll=3 if part else 2)

    def remote(src, dst, ss, rs, peer):
        return pltpu.make_async_remote_copy(
            src_ref=src, dst_ref=dst, send_sem=ss, recv_sem=rs, device_id=peer, device_id_type=MESH
        )

    def take(like, rs):
        remote(like, like, rs, rs, mate_ids[0]).wait_recv()

    def left(like, ss):
        remote(like, like, ss, ss, mate_ids[0]).wait_send()

    def each(ci, body):
        first, count = CHUNKS[ci]

        def step(i, carry):
            body(i)
            return carry

        lax.fori_loop(first, first + count, step, 0)

    def cut(ci):
        first, count = CHUNKS[ci]
        return slice(first, first + count)

    def send_max(o, ci):
        w = cut(ci)
        for k, (mx, mc) in enumerate(mates):
            remote(enc.at[o, mc, mx, w], rx.at[o, k, w], x_ss.at[o], x_rs.at[o, ci], mate_ids[k]).start()

    def merge_x(o, ci):
        w = cut(ci)
        take(rx.at[o, :, w], x_rs.at[o, ci])

        def body(i):
            hx[o, i] = top(enc[o, core, x, i], *[rx[o, k, i] for k in range(7)])

        each(ci, body)
        for k in range(3):
            remote(hx.at[o, w], rz.at[o, k, w], z_ss.at[o], z_rs.at[o, ci], z_peers[k]).start()

    def merge_z(o, ci):
        w = cut(ci)
        take(rz.at[o, :, w], z_rs.at[o, ci])

        def body(i):
            res[o, core, x, i] = top(hx[o, i], rz[o, 0, i], rz[o, 1, i], rz[o, 2, i])

        each(ci, body)
        mine = res.at[o, core, x, w]
        for k in range(7):
            remote(mine, mine, xa_ss.at[o], xa_rs.at[o, ci], mate_ids[k]).start()

        if o == 0 and ci >= 3:
            has, slab_id = (has_below, lax.rem(slab + 15, 16)) if ci == 3 else (has_above, lax.rem(slab + 1, 16))
            spot = hv.at[1, 4 - ci, core, x]

            def halo():
                for peer in group(slab_id):
                    remote(mine, spot, halo_ss.at[1, ci - 3, 0], halo_rs.at[1, ci - 3, 0], peer).start()

            pl.when(has)(halo)

    def finish(o, ci):
        take(rx.at[o, :, cut(ci)], xa_rs.at[o, ci])

        def body(i):
            if ci == 0:
                p = i + 6
            elif ci < 3:
                p = pair_plane(i - 4, 3)
            else:
                p = pair_plane(i - 10, 0)
            for h in range(2):
                for q in range(4):
                    row = 64 * h + 16 * q
                    if o == 0:
                        u[p + 3, 8 + row : 24 + row] = decode(res[o, h, q, i])
                    else:
                        out[p, row : row + 16] = res[o, h, q, i]

        each(ci, body)

    def to_below(o):
        if o == 0:
            moves = [
                (vst.at[0, core], hv.at[0, 1, core]),
                (sst.at[0, core], hs.at[1, core]),
                (reward.at[:, 0:2], rw.at[:, NP + 2 : NP + 4]),
            ]
        else:
            moves = [(res.at[0, :, :, 10:13], hv.at[1, 1])]
        return [remote(f, t, halo_ss.at[o, 0, i], halo_rs.at[o, 0, i], below) for i, (f, t) in enumerate(moves)]

    def to_above(o):
        if o == 0:
            moves = [
                (vst.at[1, core], hv.at[0, 0, core]),
                (sst.at[1, core], hs.at[0, core]),
                (reward.at[:, NP - 2 : NP], rw.at[:, 0:2]),
            ]
        else:
            moves = [(res.at[0, :, :, 13:16], hv.at[1, 0])]
        return [remote(f, t, halo_ss.at[o, 1, i], halo_rs.at[o, 1, i], above) for i, (f, t) in enumerate(moves)]

    def to_mate(side):
        moves = [(hv.at[0, side, core], hv.at[0, side, core]), (hs.at[side, core], hs.at[side, core])]
        return [remote(f, t, pass_ss.at[side, i], pass_rs.at[side, i], mate_ids[-1]) for i, (f, t) in enumerate(moves)]

    def pass_on(side):
        def go():
            halves = to_above(0) if side == 0 else to_below(0)
            for half, copy in zip(halves, to_mate(side)):
                half.wait_recv()
                copy.start()

        pl.when(has_below if side == 0 else has_above)(go)

    def start_all(copies):
        for copy in copies:
            copy.start()

    def send_low(o):
        pl.when(has_below)(lambda: start_all(to_below(o)))

    def send_high(o):
        pl.when(has_above)(lambda: start_all(to_above(o)))

    def take_halo(o, side):
        def wait():
            copies = to_above(o) if side == 0 else to_below(o)
            if o == 0:
                copies = to_mate(side) + copies[2:]
            for copy in copies:
                copy.wait_recv()

        pl.when(has_below if side == 0 else has_above)(wait)

        def body(i, carry):
            p = i - 3 if side == 0 else i + NP
            keep = inside(p)
            for h in range(2):
                for q in range(4):
                    row = 8 + 64 * h + 16 * q
                    u[p + 3, row : row + 16] = jnp.where(keep[0:16], decode(hv[o, side, h, q, i]), 0.0)
            return carry

        lax.fori_loop(0, 3, body, 0)
        if o == 0:

            def pace(i, carry):
                p = i - 2 if side == 0 else i + NP
                for r0 in range(0, NY, BLK):
                    sp[p + 2, r0 : r0 + BLK] = decode_speed(hs[side, r0 // 64, i, r0 % 64 : r0 % 64 + BLK])
                return carry

            lax.fori_loop(0, 2, pace, 0)

    loads[0].wait()

    def stage(i, carry):
        for side in range(2):
            p = i if side == 0 else i + NP - 3
            for h in range(2):
                for q in range(4):
                    row = 8 + 64 * h + 16 * q
                    vst[side, h, q, i] = encode(u[p + 3, row : row + 16])
        return carry

    lax.fori_loop(0, 3, stage, 0)
    loads[1].wait()

    def stage_speed(i, carry):
        for side in range(2):
            p = i if side == 0 else i + NP - 2
            for r0 in range(0, NY, BLK):
                sst[side, r0 // 64, i, r0 % 64 : r0 % 64 + BLK] = encode_speed(sp[p + 2, r0 : r0 + BLK])
        return carry

    lax.fori_loop(0, 2, stage_speed, 0)
    pl.semaphore_wait(barrier, greeted)
    pl.semaphore_signal(far, inc=1, device_id=z_peers[1], device_id_type=MESH)
    send_low(0)
    send_high(0)
    loads[2].wait()

    def inner(o):
        for step in range(3):
            sweep(step, 4 + step, 12 - step, o, 0)
        send_max(o, 0)

    def middle(o, side):
        for step in range(3):
            sweep(step, 3 * side, 3 * side + 3, o, 1)
        send_max(o, 1 + side)

    def face(o, side):
        take_halo(o, side)
        for step in range(3):
            sweep(step, 3 * side, 3 * side + 3, o, 2)
        send_max(o, 3 + side)

    inner(0)
    middle(0, 0)
    middle(0, 1)
    pl.semaphore_wait(far, 1)
    pass_on(0)
    pass_on(1)
    merge_x(0, 0)
    face(0, 0)
    merge_x(0, 1)
    face(0, 1)
    for ci in (2, 3, 4):
        merge_x(0, ci)
    for ci in range(5):
        merge_z(0, ci)
    for ci in range(3):
        finish(0, ci)

    for step in range(2):
        sweep(step, 4 + step, 12 - step, 1, 0)
    finish(0, 3)
    sweep(2, 6, 10, 1, 0)
    send_max(1, 0)
    middle(1, 0)
    finish(0, 4)
    middle(1, 1)
    merge_x(1, 0)
    face(1, 1)
    merge_x(1, 1)
    face(1, 0)
    order = (0, 1, 2, 4, 3)
    for ci in order[2:]:
        merge_x(1, ci)
    for ci in order:
        merge_z(1, ci)
    for ci in order:
        finish(1, ci)

    for o in range(2):
        left(rx.at[o], x_ss.at[o])
        left(rz.at[o], z_ss.at[o])
        left(rx.at[o], xa_ss.at[o])

        def low_left():
            for copy in to_below(o) + (to_mate(0) if o == 0 else []):
                copy.wait_send()

        def high_left():
            for copy in to_above(o) + (to_mate(1) if o == 0 else []):
                copy.wait_send()

        pl.when(has_below)(low_left)
        pl.when(has_above)(high_left)


def body(value, speed, reward, ctrl_set, drift_sets, diffusion_sets):
    hbm = pl.BlockSpec(memory_space=pl.ANY)
    dma = pltpu.SemaphoreType.DMA
    n = len(CHUNKS)
    code = pl.pallas_call(
        kernel,
        out_shape=pltpu.VMEM((NP, NY, NZ), I16),
        in_specs=[hbm] * 6,
        out_specs=pl.BlockSpec(memory_space=pltpu.VMEM),
        scratch_shapes=[
            pltpu.SMEM((2,), jnp.int32),
            pltpu.SMEM((3, 16), F32),
            pltpu.SMEM((3, 16), F32),
            pltpu.VMEM((NP + 6, NY + 16, NZ), F32),
            pltpu.VMEM((NP + 4, NY, NZ), F32),
            pltpu.VMEM((2, NP + 4, NY, NZ), jnp.bfloat16),
            pltpu.VMEM((2, NP + 4, NY, NZ), F32),
            pltpu.VMEM((2, NP + 4, NY + 16, NZ), F32),
            pltpu.VMEM((2, NP + 2, NY + 16, NZ), F32),
            pltpu.VMEM((2, 2, 4, NP, 16, NZ), I16),
            pltpu.VMEM((2, 7, NP, 16, NZ), I16),
            pltpu.VMEM((2, NP, 16, NZ), I16),
            pltpu.VMEM((2, 3, NP, 16, NZ), I16),
            pltpu.VMEM((2, 2, 4, NP, 16, NZ), I16),
            pltpu.VMEM((2, 2, 4, 3, 16, NZ), I16),
            pltpu.VMEM((2, 2, 2, 4, 3, 16, NZ), I16),
            pltpu.VMEM((2, 2, 2, NY // 2, NZ), I16),
            pltpu.VMEM((2, 2, 2, NY // 2, NZ), I16),
            dma((6,)),
            dma((2, 2, 3)), dma((2, 2, 3)),
            dma((2, 2)), dma((2, 2)),
            dma((2,)), dma((2, n)),
            dma((2,)), dma((2, n)),
            dma((2,)), dma((2, n)),
            pltpu.SemaphoreType.REGULAR,
        ],
        compiler_params=pltpu.CompilerParams(collective_id=0, has_side_effects=True),
        name="hjb",
    )(ctrl_set, drift_sets.T, diffusion_sets.T, value, speed, reward)
    return decode(code)


def solution(mesh):
    in_specs = (
        P("slab", None, None),
        P("slab", None, None),
        P("ctrl", "slab", None, None),
        P("ctrl"),
        P(),
        P(),
    )
    out_specs = P("slab", None, None)
    return jax.shard_map(body, mesh=mesh, in_specs=in_specs, out_specs=out_specs, check_vma=False)
```

```python
import functools

import jax
import jax.numpy as jnp
from jax import lax
from jax.experimental import pallas as pl
from jax.experimental.pallas import tpu as pltpu
from jax.sharding import PartitionSpec as P

MESH = pl.DeviceIdType.MESH
F32 = jnp.float32
I16 = jnp.int16
OUTER = 2
NP = 16
NY = 128
NZ = 128
BLK = 32
KEY = 32767.0 / 11.45**0.25
SKEY = 32767.0 / 0.376
CHUNKS = ((0, 4), (4, 3), (7, 3), (10, 3), (13, 3))
OFFSETS = tuple((dx, dc) for dx in (2, 1, 3, 0) for dc in range(2) if dx or dc)


def encode(v):
    root = lax.rsqrt(lax.rsqrt(jnp.maximum(jnp.abs(v), 1e-30)))
    size = root * KEY + 0.5
    return jnp.where(v < 0.0, -size, size).astype(jnp.int32).astype(I16)


def decode(code):
    g = code.astype(jnp.int32).astype(F32) * (1.0 / KEY)
    return (g * jnp.abs(g)) * (g * g)


def encode_speed(s):
    t = (s - 0.625) * SKEY
    return jnp.where(t < 0.0, t - 0.5, t + 0.5).astype(jnp.int32).astype(I16)


def decode_speed(code):
    return code.astype(jnp.int32).astype(F32) * (1.0 / SKEY) + 0.625


def top(*codes):
    best = codes[0].astype(jnp.int32).astype(F32)
    for code in codes[1:]:
        best = jnp.maximum(best, code.astype(jnp.int32).astype(F32))
    return best.astype(jnp.int32).astype(I16)


def pair_plane(j, base):
    return j + base + (j // 3) * (10 - 2 * base)


def kernel(
    cset_in, drift_in, diff_in, value, speed, reward, out,
    cset, drift, diff, u, sp, rw, wide, f1, f2, enc, rx, hx, rz, res, vst, hv, sst, hs,
    load_sem, halo_ss, halo_rs, pass_ss, pass_rs, x_ss, x_rs, z_ss, z_rs, xa_ss, xa_rs, far,
):
    slab = lax.axis_index("slab")
    ctrl = lax.axis_index("ctrl")
    core = lax.rem(ctrl, 2)
    x = lax.rem(ctrl // 2, 4)
    z = ctrl // 8

    def at(z, x, core):
        return {"slab": slab, "ctrl": (z * 4 + x) * 2 + core}

    mates = [(lax.rem(x + dx, 4), lax.rem(core + dc, 2)) for dx, dc in OFFSETS]
    mate_ids = [at(z, mx, mc) for mx, mc in mates]
    z_peers = [at(lax.rem(z + k, 4), x, core) for k in (2, 1, 3)]
    below = {"slab": lax.rem(slab + 15, 16), "ctrl": ctrl}
    above = {"slab": lax.rem(slab + 1, 16), "ctrl": ctrl}
    has_below = slab > 0
    has_above = slab < 15
    greeted = jnp.where(has_below, 1, 0) + jnp.where(has_above, 1, 0) + 9

    barrier = pltpu.get_barrier_semaphore()

    def greet(peer):
        pl.semaphore_signal(barrier, inc=1, device_id=peer, device_id_type=MESH)

    pl.when(has_below)(lambda: greet(below))
    pl.when(has_above)(lambda: greet(above))
    for peer in z_peers[1:] + mate_ids:
        greet(peer)

    loads = [
        pltpu.make_async_copy(value, u.at[3 : 3 + NP, 8 : 8 + NY], load_sem.at[0]),
        pltpu.make_async_copy(speed, sp.at[2 : 2 + NP], load_sem.at[1]),
        pltpu.make_async_copy(reward, rw.at[:, 2 : 2 + NP], load_sem.at[2]),
        pltpu.make_async_copy(cset_in, cset, load_sem.at[3]),
        pltpu.make_async_copy(drift_in, drift, load_sem.at[4]),
        pltpu.make_async_copy(diff_in, diff, load_sem.at[5]),
    ]
    for load in loads:
        load.start()

    strip = jnp.zeros((8, NZ), F32)

    def clear(i, carry):
        u[i, 0:8] = strip
        u[i, 8 + NY : 16 + NY] = strip
        return carry

    lax.fori_loop(0, NP + 6, clear, 0)

    def clear_one(i, carry):
        for c in range(2):
            f1[c, i, 0:8] = strip
            f1[c, i, 8 + NY : 16 + NY] = strip
        return carry

    lax.fori_loop(0, NP + 4, clear_one, 0)

    def clear_two(i, carry):
        for c in range(2):
            f2[c, i, 0:8] = strip
            f2[c, i, 8 + NY : 16 + NY] = strip
        return carry

    lax.fori_loop(0, NP + 2, clear_two, 0)

    for load in loads[3:]:
        load.wait()
    a, e, pos_b, mid, total = [], [], [], [], []
    for c in range(2):
        k = cset[c]
        a.append([diff[d, k] for d in range(3)])
        b = [drift[d, k] for d in range(3)]
        e.append([jnp.abs(bd) for bd in b])
        pos_b.append(b)
        mid.append(1.0 - 2.0 * (a[c][0] + a[c][1] + a[c][2]))
        total.append(e[c][0] + e[c][1] + e[c][2])

    lane = lax.broadcasted_iota(jnp.int32, (BLK, NZ), 1)
    not_last = lane < NZ - 1
    not_first = lane > 0

    def neighbours(src, p, r0):
        here = src[p, 8 + r0 : 8 + r0 + BLK]
        ahead = [
            src[p + 1, 8 + r0 : 8 + r0 + BLK],
            src[p, 9 + r0 : 9 + r0 + BLK],
            jnp.where(not_last, pltpu.roll(here, NZ - 1, 1), 0.0),
        ]
        behind = [
            src[p - 1, 8 + r0 : 8 + r0 + BLK],
            src[p, 7 + r0 : 7 + r0 + BLK],
            jnp.where(not_first, pltpu.roll(here, 1, 1), 0.0),
        ]
        sums = [f + g for f, g in zip(ahead, behind)]
        return here, ahead, behind, sums

    def advance(step, p, r0, o):
        pace = sp[p + 2, r0 : r0 + BLK]
        if step == 0:
            shared = neighbours(u, p + 3, r0)
        results = []
        for c in range(2):
            if step == 0:
                here, ahead, behind, sums = shared
            elif step == 1:
                here, ahead, behind, sums = neighbours(f1.at[c], p + 2, r0)
            else:
                here, ahead, behind, sums = neighbours(f2.at[c], p + 1, r0)
            if step == 0 and o == 0:
                pay = rw[c, p + 2, r0 : r0 + BLK].astype(F32)
                wide[c, p + 2, r0 : r0 + BLK] = pay
            else:
                pay = wide[c, p + 2, r0 : r0 + BLK]
            wind = [
                e[c][d] * jnp.where(jnp.full((BLK, NZ), pos_b[c][d], F32) > 0.0, ahead[d], behind[d])
                for d in range(3)
            ]
            spread = (a[c][0] * sums[0] + a[c][1] * sums[1]) + (a[c][2] * sums[2] + mid[c] * here)
            flow = (wind[0] + wind[1]) + (wind[2] - total[c] * here)
            results.append((spread + pay) + pace * flow)
        return results

    def inside(p):
        lost = jnp.logical_or(jnp.logical_and(p < 0, slab == 0), jnp.logical_and(p >= NP, slab == 15))
        return jnp.full((BLK, NZ), jnp.where(lost, 0, 1), jnp.int32) > 0

    def sweep(step, low, high, o, part):
        def body(j, carry):
            if part == 0:
                p, pos = j, j - 6
            elif part == 1:
                p, pos = pair_plane(j, step + 1), j + 4
            else:
                p, pos = pair_plane(j, step - 2), j + 10
                keep = inside(p)
            for r0 in range(0, NY, BLK):
                both = advance(step, p, r0, o)
                if step < 2:
                    dst, off = (f1, 2) if step == 0 else (f2, 1)
                    for c in range(2):
                        dst[c, p + off, 8 + r0 : 8 + r0 + BLK] = jnp.where(keep, both[c], 0.0) if part == 2 else both[c]
                else:
                    code = encode(jnp.maximum(both[0], both[1]))
                    for i in range(BLK // 16):
                        h, q = divmod(r0 // 16 + i, 4)
                        enc[o, h, q, pos] = code[16 * i : 16 * i + 16]
            return carry

        lax.fori_loop(low, high, body, 0, unroll=3 if part else (high - low) // 2)

    def remote(src, dst, ss, rs, peer):
        return pltpu.make_async_remote_copy(
            src_ref=src, dst_ref=dst, send_sem=ss, recv_sem=rs, device_id=peer, device_id_type=MESH
        )

    def take(like, rs):
        remote(like, like, rs, rs, mate_ids[0]).wait_recv()

    def left(like, ss):
        remote(like, like, ss, ss, mate_ids[0]).wait_send()

    def each(ci, body):
        first, count = CHUNKS[ci]

        def step(i, carry):
            body(i)
            return carry

        lax.fori_loop(first, first + count, step, 0)

    def cut(ci):
        first, count = CHUNKS[ci]
        return slice(first, first + count)

    def send_max(o, ci):
        w = cut(ci)
        for k, (mx, mc) in enumerate(mates):
            remote(enc.at[o, mc, mx, w], rx.at[o, k, w], x_ss.at[o], x_rs.at[o, ci], mate_ids[k]).start()

    def merge_x(o, ci):
        w = cut(ci)
        take(rx.at[o, :, w], x_rs.at[o, ci])

        def body(i):
            hx[o, i] = top(enc[o, core, x, i], *[rx[o, k, i] for k in range(7)])

        each(ci, body)
        for k in range(3):
            remote(hx.at[o, w], rz.at[o, k, w], z_ss.at[o], z_rs.at[o, ci], z_peers[k]).start()

    def merge_z(o, ci):
        w = cut(ci)
        take(rz.at[o, :, w], z_rs.at[o, ci])

        def body(i):
            res[o, core, x, i] = top(hx[o, i], rz[o, 0, i], rz[o, 1, i], rz[o, 2, i])

        each(ci, body)
        mine = res.at[o, core, x, w]
        for k in range(7):
            remote(mine, mine, xa_ss.at[o], xa_rs.at[o, ci], mate_ids[k]).start()

    def finish(o, ci):
        take(rx.at[o, :, cut(ci)], xa_rs.at[o, ci])

        def body(i):
            if ci == 0:
                p = i + 6
            elif ci < 3:
                p = pair_plane(i - 4, 3)
            else:
                p = pair_plane(i - 10, 0)
            for h in range(2):
                for q in range(4):
                    row = 64 * h + 16 * q
                    if o == 0:
                        u[p + 3, 8 + row : 24 + row] = decode(res[o, h, q, i])
                    else:
                        out[p, row : row + 16] = res[o, h, q, i]

        each(ci, body)

    def to_below(o):
        if o == 0:
            moves = [
                (vst.at[0, core], hv.at[0, 1, core]),
                (sst.at[0, core], hs.at[1, core]),
                (reward.at[:, 0:2], rw.at[:, NP + 2 : NP + 4]),
            ]
        else:
            moves = [(res.at[0, :, :, 10:13], hv.at[1, 1])]
        return [remote(f, t, halo_ss.at[o, 0, i], halo_rs.at[o, 0, i], below) for i, (f, t) in enumerate(moves)]

    def to_above(o):
        if o == 0:
            moves = [
                (vst.at[1, core], hv.at[0, 0, core]),
                (sst.at[1, core], hs.at[0, core]),
                (reward.at[:, NP - 2 : NP], rw.at[:, 0:2]),
            ]
        else:
            moves = [(res.at[0, :, :, 13:16], hv.at[1, 0])]
        return [remote(f, t, halo_ss.at[o, 1, i], halo_rs.at[o, 1, i], above) for i, (f, t) in enumerate(moves)]

    def to_mate(side):
        moves = [(hv.at[0, side, core], hv.at[0, side, core]), (hs.at[side, core], hs.at[side, core])]
        return [remote(f, t, pass_ss.at[side, i], pass_rs.at[side, i], mate_ids[-1]) for i, (f, t) in enumerate(moves)]

    def pass_on(side):
        def go():
            halves = to_above(0) if side == 0 else to_below(0)
            for half, copy in zip(halves, to_mate(side)):
                half.wait_recv()
                copy.start()

        pl.when(has_below if side == 0 else has_above)(go)

    def start_all(copies):
        for copy in copies:
            copy.start()

    def send_low(o):
        pl.when(has_below)(lambda: start_all(to_below(o)))

    def send_high(o):
        pl.when(has_above)(lambda: start_all(to_above(o)))

    def take_halo(o, side):
        def wait():
            copies = to_above(o) if side == 0 else to_below(o)
            if o == 0:
                copies = to_mate(side) + copies[2:]
            for copy in copies:
                copy.wait_recv()

        pl.when(has_below if side == 0 else has_above)(wait)

        def body(i, carry):
            p = i - 3 if side == 0 else i + NP
            keep = inside(p)
            for h in range(2):
                for q in range(4):
                    row = 8 + 64 * h + 16 * q
                    u[p + 3, row : row + 16] = jnp.where(keep[0:16], decode(hv[o, side, h, q, i]), 0.0)
            return carry

        lax.fori_loop(0, 3, body, 0)
        if o == 0:

            def pace(i, carry):
                p = i - 2 if side == 0 else i + NP
                for r0 in range(0, NY, BLK):
                    sp[p + 2, r0 : r0 + BLK] = decode_speed(hs[side, r0 // 64, i, r0 % 64 : r0 % 64 + BLK])
                return carry

            lax.fori_loop(0, 2, pace, 0)

    loads[0].wait()

    def stage(i, carry):
        for side in range(2):
            p = i if side == 0 else i + NP - 3
            for h in range(2):
                for q in range(4):
                    row = 8 + 64 * h + 16 * q
                    vst[side, h, q, i] = encode(u[p + 3, row : row + 16])
        return carry

    lax.fori_loop(0, 3, stage, 0)
    loads[1].wait()

    def stage_speed(i, carry):
        for side in range(2):
            p = i if side == 0 else i + NP - 2
            for r0 in range(0, NY, BLK):
                sst[side, r0 // 64, i, r0 % 64 : r0 % 64 + BLK] = encode_speed(sp[p + 2, r0 : r0 + BLK])
        return carry

    lax.fori_loop(0, 2, stage_speed, 0)
    pl.semaphore_wait(barrier, greeted)
    pl.semaphore_signal(far, inc=1, device_id=z_peers[1], device_id_type=MESH)
    send_low(0)
    send_high(0)
    loads[2].wait()

    def inner(o):
        for step in range(3):
            sweep(step, 4 + step, 12 - step, o, 0)
        send_max(o, 0)

    def middle(o, side):
        for step in range(3):
            sweep(step, 3 * side, 3 * side + 3, o, 1)
        send_max(o, 1 + side)

    def face(o, side):
        take_halo(o, side)
        for step in range(3):
            sweep(step, 3 * side, 3 * side + 3, o, 2)
        send_max(o, 3 + side)

    inner(0)
    middle(0, 0)
    middle(0, 1)
    pl.semaphore_wait(far, 1)
    pass_on(0)
    pass_on(1)
    merge_x(0, 0)
    face(0, 0)
    merge_x(0, 1)
    face(0, 1)
    for ci in (2, 3, 4):
        merge_x(0, ci)
    for ci in range(5):
        merge_z(0, ci)
    for ci in range(3):
        finish(0, ci)

    for step in range(2):
        sweep(step, 4 + step, 12 - step, 1, 0)
    finish(0, 3)
    send_low(1)
    sweep(2, 6, 10, 1, 0)
    send_max(1, 0)
    middle(1, 0)
    finish(0, 4)
    send_high(1)
    middle(1, 1)
    merge_x(1, 0)
    face(1, 1)
    merge_x(1, 1)
    face(1, 0)
    order = (0, 1, 2, 4, 3)
    for ci in order[2:]:
        merge_x(1, ci)
    for ci in order:
        merge_z(1, ci)
    for ci in order:
        finish(1, ci)

    for o in range(2):
        left(rx.at[o], x_ss.at[o])
        left(rz.at[o], z_ss.at[o])
        left(rx.at[o], xa_ss.at[o])

        def low_left():
            for copy in to_below(o) + (to_mate(0) if o == 0 else []):
                copy.wait_send()

        def high_left():
            for copy in to_above(o) + (to_mate(1) if o == 0 else []):
                copy.wait_send()

        pl.when(has_below)(low_left)
        pl.when(has_above)(high_left)


def body(value, speed, reward, ctrl_set, drift_sets, diffusion_sets):
    hbm = pl.BlockSpec(memory_space=pl.ANY)
    dma = pltpu.SemaphoreType.DMA
    n = len(CHUNKS)
    code = pl.pallas_call(
        kernel,
        out_shape=pltpu.VMEM((NP, NY, NZ), I16),
        in_specs=[hbm] * 6,
        out_specs=pl.BlockSpec(memory_space=pltpu.VMEM),
        scratch_shapes=[
            pltpu.SMEM((2,), jnp.int32),
            pltpu.SMEM((3, 16), F32),
            pltpu.SMEM((3, 16), F32),
            pltpu.VMEM((NP + 6, NY + 16, NZ), F32),
            pltpu.VMEM((NP + 4, NY, NZ), F32),
            pltpu.VMEM((2, NP + 4, NY, NZ), jnp.bfloat16),
            pltpu.VMEM((2, NP + 4, NY, NZ), F32),
            pltpu.VMEM((2, NP + 4, NY + 16, NZ), F32),
            pltpu.VMEM((2, NP + 2, NY + 16, NZ), F32),
            pltpu.VMEM((2, 2, 4, NP, 16, NZ), I16),
            pltpu.VMEM((2, 7, NP, 16, NZ), I16),
            pltpu.VMEM((2, NP, 16, NZ), I16),
            pltpu.VMEM((2, 3, NP, 16, NZ), I16),
            pltpu.VMEM((2, 2, 4, NP, 16, NZ), I16),
            pltpu.VMEM((2, 2, 4, 3, 16, NZ), I16),
            pltpu.VMEM((2, 2, 2, 4, 3, 16, NZ), I16),
            pltpu.VMEM((2, 2, 2, NY // 2, NZ), I16),
            pltpu.VMEM((2, 2, 2, NY // 2, NZ), I16),
            dma((6,)),
            dma((2, 2, 3)), dma((2, 2, 3)),
            dma((2, 2)), dma((2, 2)),
            dma((2,)), dma((2, n)),
            dma((2,)), dma((2, n)),
            dma((2,)), dma((2, n)),
            pltpu.SemaphoreType.REGULAR,
        ],
        compiler_params=pltpu.CompilerParams(collective_id=0, has_side_effects=True),
        name="hjb",
    )(ctrl_set, drift_sets.T, diffusion_sets.T, value, speed, reward)
    return decode(code)


def solution(mesh):
    in_specs = (
        P("slab", None, None),
        P("slab", None, None),
        P("ctrl", "slab", None, None),
        P("ctrl"),
        P(),
        P(),
    )
    out_specs = P("slab", None, None)
    return jax.shard_map(body, mesh=mesh, in_specs=in_specs, out_specs=out_specs, check_vma=False)
```
